128 devices in a mesh: seq: 16 (over z, y), tensor: 8 (over x, core).
Axes of the slice: x: 4, y: 4, z: 4, core: 2. Of those that a mesh axis runs over, the one named last changes fastest.
Arguments:
- hidden_in: float32 [4096, 3840], P('seq'), may hold values from -6 to 6
- query_proj: float32 [3840, 4096], P(None, 'tensor'), may hold values from -0.09375 to 0.09375
- key_proj: float32 [3840, 2048], P(None, 'tensor'), may hold values from -0.09375 to 0.09375
- value_proj: float32 [3840, 2048], P(None, 'tensor'), may hold values from -0.09375 to 0.09375
- query_gain: float32 [256], replicated, may hold values from 0.1 to 1.9
- key_gain: float32 [256], replicated, may hold values from 0.1 to 1.9
- segment_ids: int32 [4096], replicated, may hold values from 0 to 3, never falling along the last dimension, each value on 1 to 2048 neighbouring positions
- grad_out: float32 [4096, 4096], P('seq', 'tensor'), may hold values from -6 to 6
Outputs:
- attended: float32 [4096, 4096], P('seq', 'tensor')
- grad_input: float32 [4096, 3840], P('seq', 'tensor')
- grad_query: float32 [3840, 4096], P('seq', 'tensor')
- grad_key: float32 [3840, 2048], P('seq', 'tensor')
- grad_value: float32 [3840, 2048], P('seq', 'tensor')
The draws below stay inside these ranges and needn't reach their ends.
Inputs may be any that keep to these rules, and one draw needn't show every extreme that they name: `segment_ids`: segment ids never fall along the transcript; each of the 4 documents holds 1 to 2048 tokens and one holds exactly 2048.
All inputs are finite; a program needn't handle non-finite values.
Results may differ from the reference program's by a relative error of at most 0.0003.
Values sent between devices are 32-bit elements; how exact they have to be, the bound alone decides.
A program may use at most 128 MiB of HBM per device.

```python
import math
import jax
import jax.numpy as jnp
import numpy as np
from jax import lax

D = 3840
HEADS = 16
KV_HEADS = 8
HEAD_DIM = 256
WINDOW = 1024
TOK_DEV = 256
SEQ = 4096


def steps_of(own_key, extent, split, least, largest):
    level = 1.0
    for position, shards_of in split:
        steps = jax.random.uniform(jax.random.fold_in(jax.random.fold_in(own_key, 6), position), (shards_of,), jnp.float32, least / len(split), largest / len(split))
        level = level * jnp.repeat(jnp.exp(steps), extent[position] // shards_of).reshape((-1,) + (1,) * (len(extent) - 1 - position))
    return level


def length_profile(count, total, bound, lean):
    portions = [(1 << 20) // math.isqrt(standing ** lean) + 1 for standing in range(2, count + 1)]
    surplus, given = total - bound - (count - 1), [1] * (count - 1)
    while surplus > 0:
        candidates = [i for i in range(count - 1) if given[i] < bound]
        mass, left = sum([portions[i] for i in candidates]), surplus
        for i in candidates:
            more = min(bound - given[i], max(1, left * portions[i] // mass), surplus)
            given[i] = given[i] + more
            surplus = surplus - more
    return np.array([bound] + given)


def uneven(rng, count, total, most, lean):
    if count == 2:
        one = jax.random.randint(rng, (), max(1, total - most), min(most, total - 1) + 1)
        return jnp.stack([one, total - one])
    tallies = jnp.asarray(length_profile(count, total, most, lean), jnp.int32)
    twos = (count - 1) // 2
    source_of, sink = tallies[1:1 + 2 * twos:2], tallies[2:2 + 2 * twos:2]
    margin = jnp.minimum(source_of - 1, most - sink)
    passed = jax.random.randint(jax.random.fold_in(rng, 1), (twos,), 0, 1 << 20) % (margin + 1)
    tallies = tallies.at[1:1 + 2 * twos:2].set(source_of - passed).at[2:2 + 2 * twos:2].set(sink + passed)
    return tallies[jax.random.permutation(jax.random.fold_in(rng, 2), count)]


def gaussian(key, shape, scale, limit, split=(), kind=jnp.bfloat16):
    result = jax.random.normal(key, shape, jnp.float32) * scale
    if len(split) > 0:
        result = steps_of(key, shape, split, -0.22, 0.18) * result
    return jnp.clip(result, min=-limit, max=limit).astype(kind)


def setup_inputs(seed: int = 0) -> dict:
    key_of = jax.random.split(jax.random.key(seed), 9)
    hidden_in = gaussian(key_of[0], (SEQ, D), 1.0, 6.0, ((0, 16),), jnp.float32)
    query_proj = gaussian(key_of[1], (D, HEADS * HEAD_DIM), D ** -0.5, 0.09375, ((1, 8),), jnp.float32)
    key_proj = gaussian(key_of[2], (D, KV_HEADS * HEAD_DIM), D ** -0.5, 0.09375, ((1, 8),), jnp.float32)
    value_proj = gaussian(key_of[3], (D, KV_HEADS * HEAD_DIM), D ** -0.5, 0.09375, ((1, 8),), jnp.float32)
    query_gain = jnp.clip(1.0 + 0.18 * jax.random.normal(key_of[4], (HEAD_DIM,), jnp.float32), 0.1, 1.9)
    key_gain = jnp.clip(1.0 + 0.18 * jax.random.normal(key_of[5], (HEAD_DIM,), jnp.float32), 0.1, 1.9)
    segment_ids = jnp.searchsorted(jnp.cumsum(uneven(key_of[6], 4, SEQ, SEQ // 2, 1)), jnp.arange(SEQ), side="right").astype(jnp.int32)
    grad_out = gaussian(key_of[7], (SEQ, HEADS * HEAD_DIM), 1.0, 6.0, ((0, 16), (1, 8)), jnp.float32)
    return {"hidden_in": hidden_in, "query_proj": query_proj, "key_proj": key_proj, "value_proj": value_proj, "query_gain": query_gain, "key_gain": key_gain, "segment_ids": segment_ids, "grad_out": grad_out}


highest = lax.Precision.HIGHEST
epsilon = 1e-06

def rms_gain(vector, scaling):
    mean_sq = lax.optimization_barrier(jnp.mean(vector * vector, axis=-1, keepdims=True))
    return vector * lax.rsqrt(mean_sq + epsilon) * scaling

def rotate(vector, cosine, sines):
    middle = vector.shape[-1] // 2
    turned = jnp.concatenate([-vector[..., middle:], vector[..., :middle]], axis=-1)
    return vector * cosine + turned * sines

def rope_tables(positions, head_width):
    middle = head_width // 2
    exponent = 2.0 * jnp.arange(middle).astype(jnp.float32) / head_width
    frequency = 10000.0 ** (-exponent)
    angles = positions.astype(jnp.float32)[:, None] * frequency[None, :]
    angles = jnp.concatenate([angles, angles], axis=-1)
    return (jnp.cos(angles)[:, None, :], jnp.sin(angles)[:, None, :])

def forward(hidden_in, query_proj, key_proj, value_proj, query_gain, key_gain, segment_ids):
    per_kv = HEADS // KV_HEADS
    queries = jnp.dot(hidden_in, query_proj, precision=highest).reshape(SEQ, KV_HEADS, per_kv, HEAD_DIM)
    key_raw = jnp.dot(hidden_in, key_proj, precision=highest).reshape(SEQ, KV_HEADS, HEAD_DIM)
    values = jnp.dot(hidden_in, value_proj, precision=highest).reshape(SEQ, KV_HEADS, HEAD_DIM)
    cosine, sines = rope_tables(jnp.arange(SEQ).astype(jnp.int32), HEAD_DIM)
    q_rot = rotate(rms_gain(queries, query_gain), cosine[:, None], sines[:, None])
    k_rot = rotate(rms_gain(key_raw, key_gain), cosine, sines)
    k_pad = jnp.concatenate([jnp.zeros((WINDOW, KV_HEADS, HEAD_DIM), jnp.float32), k_rot], axis=0)
    v_pad = jnp.concatenate([jnp.zeros((WINDOW, KV_HEADS, HEAD_DIM), jnp.float32), values], axis=0)
    seg_pad = jnp.concatenate([jnp.full((WINDOW,), -1, jnp.int32), segment_ids.astype(jnp.int32)])
    factor = HEAD_DIM ** (-0.5)

    def one_block(first_row):
        q_block = lax.dynamic_slice_in_dim(q_rot, first_row, TOK_DEV, 0)
        k_block = lax.dynamic_slice_in_dim(k_pad, first_row, TOK_DEV + WINDOW, 0)
        v_block = lax.dynamic_slice_in_dim(v_pad, first_row, TOK_DEV + WINDOW, 0)
        query_seg = lax.dynamic_slice_in_dim(segment_ids.astype(jnp.int32), first_row, TOK_DEV, 0)
        key_seg = lax.dynamic_slice_in_dim(seg_pad, first_row, TOK_DEV + WINDOW, 0)
        query_pos = first_row + jnp.arange(TOK_DEV).astype(jnp.int32)
        key_pos = first_row - WINDOW + jnp.arange(TOK_DEV + WINDOW).astype(jnp.int32)
        distance = query_pos[:, None] - key_pos[None, :]
        allowed = (key_pos[None, :] >= 0) & (distance >= 0) & (distance < WINDOW) & (query_seg[:, None] == key_seg[None, :])
        scores = jnp.einsum('tkgd,skd->kgts', q_block, k_block, precision=highest) * factor
        weights = jnp.where(allowed, jnp.exp(scores), 0.0)
        shares = weights / lax.optimization_barrier(jnp.sum(weights, axis=-1, keepdims=True))
        return jnp.einsum('kgts,skd->tkgd', shares, v_block, precision=highest)
    starts = jnp.arange(SEQ // TOK_DEV).astype(jnp.int32) * TOK_DEV
    blocks = lax.map(one_block, starts)
    return blocks.reshape(SEQ, HEADS * HEAD_DIM)

def reference(hidden_in, query_proj, key_proj, value_proj, query_gain, key_gain, segment_ids, grad_out):

    def project_all(inputs, w_query, w_key, w_value):
        return forward(inputs, w_query, w_key, w_value, query_gain, key_gain, segment_ids)
    attended, pullback = jax.vjp(project_all, hidden_in, query_proj, key_proj, value_proj)
    grad_input, grad_query, grad_key, grad_value = pullback(grad_out)
    return (attended, grad_input, grad_query, grad_key, grad_value)
```

```python
import functools

import jax
import jax.numpy as jnp
from jax import lax
from jax.experimental import pallas as pl
from jax.experimental.pallas import tpu as pltpu
from jax.sharding import PartitionSpec as P

MESH = pl.DeviceIdType.MESH
WINDOW = 1024
EPS = 1e-06
T = 256
H = 256
D = 3840
NCH = 5
CH = D // NCH
F32, BF16 = jnp.float32, jnp.bfloat16

NN = (((1,), (0,)), ((), ()))
NT = (((1,), (1,)), ((), ()))
TN = (((0,), (0,)), ((), ()))


def split(value):
    high = value.astype(BF16)
    return high, (value - high.astype(F32)).astype(BF16)


def product(left, right, dims):
    (lh, ll), (rh, rl) = left, right
    dot = functools.partial(lax.dot_general, dimension_numbers=dims, preferred_element_type=F32)
    return dot(lh, rh) + (dot(lh, rl) + dot(ll, rh))


def rotate(u, cos, sin):
    a, b = u[:, :128], u[:, 128:]
    return jnp.concatenate([a * cos - b * sin, b * cos + a * sin], axis=1)


def unrotate(u, cos, sin):
    a, b = u[:, :128], u[:, 128:]
    return jnp.concatenate([a * cos + b * sin, b * cos - a * sin], axis=1)


def inv_rms(x):
    return lax.rsqrt(jnp.mean(x * x, axis=1, keepdims=True) + EPS)


def norm_back(x, gain, d_norm):
    r = inv_rms(x)
    gd = d_norm * gain
    return r * gd - x * (r * r * r) * jnp.mean(x * gd, axis=1, keepdims=True)


def kernel(
    hid_h, wq_h, wk_h, wv_h, grad_h, gains, seg, cos_r, sin_r,
    att_o, gin_o, gq_o, gk_o, gv_o,
    hid, wq, wk, wv, grad, raw, q2, kv, wt, dpt, dqt, contrib, rkv, prev, zr,
    hz, ht_h, ht_l, dc, part, rpart, term, r1, r2,
    lsem, kv_s, kv_r, hz_s, hz_r, hc_s, hc_r, cb_s, cb_r, pz_s, pz_r, dc_s, dc_r, pt_s, pt_r, t1_s, t1_r, t2_s, t2_r,
):
    s = lax.axis_index("seq")
    t = lax.axis_index("tensor")
    z, y = s // 4, lax.rem(s, 4)
    x, c = t // 2, lax.rem(t, 2)

    def at_z(d):
        return (lax.rem(z + d + 4, 4) * 4 + y, t)

    def at_y(d):
        return (z * 4 + lax.rem(y + d + 4, 4), t)

    def at_x(d):
        return (s, lax.rem(x + d + 4, 4) * 2 + c)

    mate = (s, x * 2 + 1 - c)

    def remote(src, dst, ssem, rsem, dev):
        return pltpu.make_async_remote_copy(
            src_ref=src, dst_ref=dst, send_sem=ssem, recv_sem=rsem, device_id=dev, device_id_type=MESH
        )

    barrier = pltpu.get_barrier_semaphore()
    partners = [at_z(1), at_z(2), at_z(3), at_y(1), at_y(2), at_y(3), at_x(1), at_x(2), at_x(3), mate]
    for dev in partners:
        pl.semaphore_signal(barrier, inc=1, device_id=dev, device_id_type=MESH)

    def columns(i):
        return pl.ds(pl.multiple_of(i * CH, CH), CH)

    def local_copy(j, i):
        if j == 0:
            return pltpu.make_async_copy(hid_h.at[:, columns(i)], hid.at[:, columns(i)], lsem.at[0, i])
        src, dst = ((wk_h, wk), (wv_h, wv), (wq_h, wq))[j - 1]
        return pltpu.make_async_copy(src.at[columns(i)], dst.at[columns(i)], lsem.at[j, i])

    for i in range(NCH):
        local_copy(0, i).start()
        local_copy(1, i).start()
    for j in (2, 3):
        for i in range(NCH):
            local_copy(j, i).start()
    grad_copy = pltpu.make_async_copy(grad_h, grad, lsem.at[4, 0])
    grad_copy.start()

    cos, sin = cos_r[...], sin_r[...]
    q_gain, k_gain = gains[0:1, :], gains[1:2, :]

    def project(j, weight, col, load_hid, load_w):
        def step(i, acc):
            if load_hid:
                local_copy(0, i).wait()
            if load_w:
                local_copy(j, i).wait()
            left = split(hid[:, columns(i)])
            right = split(weight[columns(i), col : col + H])
            return acc + product(left, right, NN)

        return lax.fori_loop(0, NCH, step, jnp.zeros((T, H), F32))

    def zhop(kind):
        return remote(kv.at[0, kind], kv.at[4, kind], kv_s.at[3, kind], kv_r.at[3, kind], at_z(1))

    def yhop(d, kind):
        return remote(
            kv.at[4 * ((y + d) // 4), kind], kv.at[d, kind], kv_s.at[d - 1, kind], kv_r.at[d - 1, kind], at_y(d)
        )

    def send_own(kind):
        zhop(kind).start()
        for d in (1, 2, 3):
            @pl.when(y + d < 4)
            def _():
                yhop(d, kind).start()

    def send_prev(kind):
        zhop(kind).wait_recv()
        for d in (1, 2, 3):
            @pl.when(y + d >= 4)
            def _():
                yhop(d, kind).start()

    key_raw = project(1, wk, 0, True, True)
    raw[2] = key_raw
    kv[0, 0] = rotate(key_raw * inv_rms(key_raw) * k_gain, cos, sin)
    pl.semaphore_wait(barrier, len(partners))
    send_own(0)
    kv[0, 1] = project(2, wv, 0, False, True)
    send_own(1)

    def query(h, load):
        q_raw = project(3, wq, h * H, False, load)
        raw[h] = q_raw
        q2[h * T : (h + 1) * T, :] = rotate(q_raw * inv_rms(q_raw) * q_gain, cos, sin) * (H ** -0.5)

    query(0, True)
    send_prev(0)
    query(1, False)
    send_prev(1)
    grad_copy.wait()

    half = pl.ds(pl.multiple_of(c * 128, 128), 128)

    def first_col(zz):
        return pl.ds(pl.multiple_of(((15 * zz) // 2) * 128, 128), 1024)

    def hidden_copy(d):
        zz = lax.rem(z + d, 4)
        return remote(hid.at[half, first_col(zz)], hz.at[d - 1, half], hz_s.at[d - 1], hz_r.at[d - 1], at_z(d))

    def hidden_mate(d):
        return remote(hz.at[d - 1, half], hz.at[d - 1, half], hc_s.at[d - 1], hc_r.at[d - 1], mate)

    for d in (1, 2, 3):
        hidden_copy(d).start()

    def q_pair():
        return split(q2[...])

    def g_pair():
        return split(jnp.concatenate([grad[:, :H], grad[:, H:]], axis=0))

    row = lax.broadcasted_iota(jnp.int32, (T, 2 * T), 0)
    col = lax.rem(lax.broadcasted_iota(jnp.int32, (T, 2 * T), 1), T)
    seg_q = seg[pl.ds(s, 1), :]
    seg_q = jnp.concatenate([seg_q, seg_q], axis=1)

    def forward(d, total, delta, out_t):
        blk = lax.rem(s - d + 16, 16)
        seg_k = jnp.broadcast_to(seg[pl.ds(blk, 1), :], (T, T)).T
        seg_k = jnp.concatenate([seg_k, seg_k], axis=1)
        dist = 256 * d + col - row
        allowed = (dist >= 0) & (dist < WINDOW) & (seg_k == seg_q) & (s - d >= 0)
        scores = product(split(kv[d, 0]), q_pair(), NT)
        weights = jnp.where(allowed, jnp.exp(scores), 0.0)
        wt[d] = weights
        v_pair = split(kv[d, 1])
        d_shares = product(v_pair, g_pair(), NT)
        dpt[d] = d_shares
        total = total + jnp.sum(weights, axis=0, keepdims=True)
        delta = delta + jnp.sum(weights * d_shares, axis=0, keepdims=True)
        return total, delta, out_t + product(v_pair, split(weights), TN)

    zero_row = jnp.zeros((1, 2 * T), F32)
    dqt[...] = jnp.zeros((H, 2 * T), F32)
    total, delta = zero_row, zero_row
    for d in (0, 4, 1, 3, 2):
        if d in (1, 2, 3):
            yhop(d, 0).wait_recv()
            yhop(d, 1).wait_recv()
        total, delta, out_t = forward(d, total, delta, dqt[...])
        dqt[...] = out_t
    inverse = 1.0 / total
    delta = delta * inverse
    attended = (dqt[...] * inverse).T
    att_o[:, :H] = attended[:T]
    att_o[:, H:] = attended[T:]

    def back_copy(d, kind):
        return remote(contrib.at[d, kind], rkv.at[d - 1, kind], cb_s.at[d - 1, kind], cb_r.at[d - 1, kind], at_y(-d))

    for d in (2, 1, 3, 4, 0):
        shares = wt[d] * inverse
        wt[d] = shares
        contrib[d, 1] = product(split(shares), g_pair(), NN)
        if d in (1, 2, 3):
            back_copy(d, 1).start()
    d_q = jnp.zeros((H, 2 * T), F32)
    for d in (2, 1, 3, 4, 0):
        d_scores = split(wt[d] * (dpt[d] - delta))
        contrib[d, 0] = product(d_scores, q_pair(), NN)
        if d in (1, 2, 3):
            back_copy(d, 0).start()
        d_q = d_q + product(split(kv[d, 0]), d_scores, TN)
    d_q = d_q.T * (H ** -0.5)

    def gather(g, d):
        w = 2 * H if g == 0 else H
        cols = pl.ds(0 if g == 0 else (g + 1) * H, w)
        return remote(dc.at[0, :, cols], dc.at[d, :, cols], dc_s.at[g, d - 1], dc_r.at[g, d - 1], at_z(d))

    for h in (0, 1):
        dc[0, :, h * H : (h + 1) * H] = norm_back(raw[h], q_gain, unrotate(d_q[h * T : (h + 1) * T], cos, sin))
    for d in (1, 2, 3):
        gather(0, d).start()

    for d in (1, 2, 3):
        hidden_copy(d).wait_recv()
        hidden_mate(d).start()

    def transpose_into(d, read):
        def step(i, carry):
            lanes = pl.multiple_of(i * 256, 256)
            high, low = split(read(lanes).T)
            ht_h[pl.ds(lanes, 256), d * T : (d + 1) * T] = high
            ht_l[pl.ds(lanes, 256), d * T : (d + 1) * T] = low
            return carry

        lax.fori_loop(0, 4, step, 0)

    base = ((15 * z) // 2) * 128
    transpose_into(0, lambda lanes: hid[:, pl.ds(pl.multiple_of(base + lanes, 128), 256)])
    for d in (1, 2, 3):
        hidden_mate(d).wait_recv()
        transpose_into(d, lambda lanes: hz[d - 1, :, pl.ds(lanes, 256)])

    def prev_copy(kind):
        return remote(prev.at[kind], zr.at[kind], pz_s.at[kind], pz_r.at[kind], at_z(-1))

    own = [None, None]
    for kind in (1, 0):
        mine, before = contrib[0, kind], contrib[4, kind]
        for d in (1, 2, 3):
            back_copy(d, kind).wait_recv()
            got = rkv[d - 1, kind]
            inside = jnp.where(y + d < 4, 1.0, 0.0).astype(F32)
            mine = mine + inside * got
            before = before + (1.0 - inside) * got
        prev[kind] = before
        contrib[0, kind] = mine
        prev_copy(kind).start()

    off = lax.rem(z, 2) * 64

    def rows_of(yy):
        return pl.ds(pl.multiple_of(off + 240 * yy, 16), 240)

    def scatter(g, d):
        return remote(part.at[d, g], rpart.at[d - 1, g], pt_s.at[g, d - 1], pt_r.at[g, d - 1], at_y(d))

    def partial(g):
        def blocks(k):
            return split(dc[k, :, g * H : (g + 1) * H])

        pieces = [blocks(k) for k in range(4)]
        right = tuple(jnp.concatenate([p[i] for p in pieces], axis=0) for i in (0, 1))
        for d in (1, 2, 3, 0):
            rows = rows_of(lax.rem(y + d, 4))
            part[d, g] = product((ht_h[rows, :], ht_l[rows, :]), right, NN)
            if d:
                scatter(g, d).start()

    for d in (1, 2, 3):
        gather(0, d).wait_recv()
    partial(0)
    partial(1)

    prev_copy(1).wait_recv()
    dc[0, :, 3 * H : 4 * H] = contrib[0, 1] + zr[1]
    for d in (1, 2, 3):
        gather(2, d).start()
    prev_copy(0).wait_recv()
    d_key = unrotate(contrib[0, 0] + zr[0], cos, sin)
    dc[0, :, 2 * H : 3 * H] = norm_back(raw[2], k_gain, d_key)
    for d in (1, 2, 3):
        gather(1, d).start()

    d_own = [split(dc[0, :, g * H : (g + 1) * H]) for g in range(4)]
    weights = [(wq, 0), (wq, H), (wk, 0), (wv, 0)]

    def input_term(tt):
        rows = pl.ds(pl.multiple_of(tt * 480, 32), 480)
        acc = None
        for g in range(4):
            w, first = weights[g]
            one = product(d_own[g], split(w[rows, first : first + H]), NT)
            acc = one if acc is None else acc + one
        return acc

    def core_copy(k):
        return remote(term.at[1, k], r1.at[k], t1_s.at[k], t1_r.at[k], mate)

    def x_copy(d):
        return remote(term.at[0, d], r2.at[d - 1], t2_s.at[d - 1], t2_r.at[d - 1], at_x(d))

    for k in (1, 2, 3, 0):
        term[1, k] = input_term(2 * lax.rem(x + k, 4) + 1 - c)
        core_copy(k).start()
    for k in (1, 2, 3, 0):
        mine = input_term(2 * lax.rem(x + k, 4) + c)
        core_copy(k).wait_recv()
        term[0, k] = mine + r1[k]
        if k:
            x_copy(k).start()

    for d in (1, 2, 3):
        gather(2, d).wait_recv()
    partial(3)
    for d in (1, 2, 3):
        gather(1, d).wait_recv()
    partial(2)

    total_in = term[0, 0]
    for k in (1, 2, 3):
        x_copy(k).wait_recv()
        total_in = total_in + r2[k - 1]
    gin_o[...] = total_in

    for g in (0, 1, 3, 2):
        acc = part[0, g]
        for d in (1, 2, 3):
            scatter(g, d).wait_recv()
            acc = acc + rpart[d - 1, g]
        if g < 2:
            gq_o[:, g * H : (g + 1) * H] = acc
        elif g == 2:
            gk_o[...] = acc
        else:
            gv_o[...] = acc

    for kind in (0, 1):
        zhop(kind).wait_send()
        prev_copy(kind).wait_send()
        for d in (1, 2, 3):
            yhop(d, kind).wait_send()
            back_copy(d, kind).wait_send()
    for d in (1, 2, 3):
        hidden_copy(d).wait_send()
        hidden_mate(d).wait_send()
        x_copy(d).wait_send()
        for g in range(3):
            gather(g, d).wait_send()
        for g in range(4):
            scatter(g, d).wait_send()
    for k in range(4):
        core_copy(k).wait_send()


def local(hidden_in, query_proj, key_proj, value_proj, query_gain, key_gain, segment_ids, grad_out):
    s = lax.axis_index("seq")
    positions = s * T + jnp.arange(T, dtype=jnp.int32)
    exponent = 2.0 * jnp.arange(H // 2).astype(F32) / H
    frequency = 10000.0 ** (-exponent)
    angles = positions.astype(F32)[:, None] * frequency[None, :]
    gains = jnp.stack([query_gain, key_gain])
    vmem = pl.BlockSpec(memory_space=pltpu.VMEM)
    hbm = pl.BlockSpec(memory_space=pl.ANY)
    V, S = pltpu.VMEM, pltpu.SemaphoreType.DMA
    shape = jax.ShapeDtypeStruct
    return pl.pallas_call(
        kernel,
        out_shape=(
            shape((T, 512), F32), shape((T, 480), F32), shape((240, 512), F32), shape((240, 256), F32), shape((240, 256), F32),
        ),
        in_specs=[hbm] * 5 + [vmem] * 4,
        out_specs=(vmem,) * 5,
        scratch_shapes=[
            V((T, D), F32), V((D, 512), F32), V((D, 256), F32), V((D, 256), F32), V((T, 512), F32),
            V((3, T, H), F32), V((2 * T, H), F32), V((5, 2, T, H), F32), V((5, T, 2 * T), F32), V((5, T, 2 * T), F32),
            V((H, 2 * T), F32), V((5, 2, T, H), F32), V((3, 2, T, H), F32), V((2, T, H), F32), V((2, T, H), F32),
            V((3, T, 1024), F32), V((1024, 1024), BF16), V((1024, 1024), BF16), V((4, T, 1024), F32),
            V((4, 4, 240, H), F32), V((3, 4, 240, H), F32), V((2, 4, T, 480), F32), V((4, T, 480), F32), V((3, T, 480), F32),
            S((5, NCH)), S((4, 2)), S((4, 2)), S((3,)), S((3,)), S((3,)), S((3,)), S((3, 2)), S((3, 2)), S((2,)), S((2,)),
            S((3, 3)), S((3, 3)), S((4, 3)), S((4, 3)), S((4,)), S((4,)), S((3,)), S((3,)),
        ],
        compiler_params=pltpu.CompilerParams(collective_id=0, has_side_effects=True, vmem_limit_bytes=63 << 20),
        cost_estimate=pl.CostEstimate(flops=24_000_000_000, bytes_accessed=40_000_000, transcendentals=700_000),
    )(
        hidden_in, query_proj, key_proj, value_proj, grad_out,
        gains, segment_ids.reshape(16, T), jnp.cos(angles), jnp.sin(angles),
    )


def solution(mesh):
    return jax.shard_map(
        local,
        mesh=mesh,
        in_specs=(
            P("seq", None), P(None, "tensor"), P(None, "tensor"), P(None, "tensor"), P(), P(), P(), P("seq", "tensor"),
        ),
        out_specs=(P("seq", "tensor"),) * 5,
        check_vma=False,
    )
```

```python
import functools

import jax
import jax.numpy as jnp
import numpy as np
from jax import lax
from jax.experimental import pallas as pl
from jax.experimental.pallas import tpu as pltpu
from jax.sharding import PartitionSpec as P

MESH = pl.DeviceIdType.MESH
WINDOW = 1024
EPS = 1e-06
T = 256
H = 256
D = 3840
NCH = 5
CH = D // NCH
F32, BF16 = jnp.float32, jnp.bfloat16

NN = (((1,), (0,)), ((), ()))
NT = (((1,), (1,)), ((), ()))
TN = (((0,), (0,)), ((), ()))


def split(value):
    high = value.astype(BF16)
    return high, (value - high.astype(F32)).astype(BF16)


def product(left, right, dims):
    (lh, ll), (rh, rl) = left, right
    dot = functools.partial(lax.dot_general, dimension_numbers=dims, preferred_element_type=F32)
    return dot(lh, rh) + (dot(lh, rl) + dot(ll, rh))


def rotate(u, cos, sin):
    a, b = u[:, :128], u[:, 128:]
    return jnp.concatenate([a * cos - b * sin, b * cos + a * sin], axis=1)


def unrotate(u, cos, sin):
    a, b = u[:, :128], u[:, 128:]
    return jnp.concatenate([a * cos + b * sin, b * cos - a * sin], axis=1)


def inv_rms(x):
    return lax.rsqrt(jnp.mean(x * x, axis=1, keepdims=True) + EPS)


def norm_back(x, gain, d_norm):
    r = inv_rms(x)
    gd = d_norm * gain
    return r * gd - x * (r * r * r) * jnp.mean(x * gd, axis=1, keepdims=True)


class Links:
    def __init__(self, send_sems, recv_sems):
        self.sems = send_sems, recv_sems
        self.copies = {}

    def add(self, name, src, dst, device):
        i = len(self.copies)
        self.copies[name] = pltpu.make_async_remote_copy(
            src_ref=src, dst_ref=dst, send_sem=self.sems[0].at[i], recv_sem=self.sems[1].at[i],
            device_id=device, device_id_type=MESH,
        )

    def start(self, *name):
        self.copies[name].start()

    def arrived(self, *name):
        self.copies[name].wait_recv()

    def finish(self):
        for copy in self.copies.values():
            copy.wait_send()


COPIES = 64


def kernel(
    hid_h, wq_h, wk_h, wv_h, grad_h, q_gain_r, k_gain_r, seg, freq_r,
    att_o, gin_o, gq_o, gk_o, gv_o,
    hid, wq, wk, wv, grad, raw, q2, kv, wt, dpt, dqt, contrib, rkv, prev, zr,
    hz, ht_h, ht_l, dc, part, fwd, rpart, term, r1, r2, lsem, send_sems, recv_sems,
):
    s = lax.axis_index("seq")
    t = lax.axis_index("tensor")
    z, y = s // 4, lax.rem(s, 4)
    x, c = t // 2, lax.rem(t, 2)

    def at_z(d):
        return (lax.rem(z + d + 4, 4) * 4 + y, t)

    def at_y(d):
        return (z * 4 + lax.rem(y + d + 4, 4), t)

    def at_x(d):
        return (s, lax.rem(x + d + 4, 4) * 2 + c)

    mate = (s, x * 2 + 1 - c)
    barrier = pltpu.get_barrier_semaphore()
    partners = [at_z(1), at_z(2), at_z(3), at_y(1), at_y(2), at_y(3), at_x(1), at_x(2), at_x(3), mate]
    for dev in partners:
        pl.semaphore_signal(barrier, inc=1, device_id=dev, device_id_type=MESH)

    links = Links(send_sems, recv_sems)
    half = pl.ds(pl.multiple_of(c * 128, 128), 128)

    def first_col(zz):
        return ((15 * zz) // 2) * 128

    for kind in (0, 1):
        links.add(("kv", 4, kind), kv.at[0, kind], kv.at[4, kind], at_z(1))
        links.add(("prev", kind), prev.at[kind], zr.at[kind], at_z(-1))
        for d in (1, 2, 3):
            links.add(("kv", d, kind), kv.at[4 * ((y + d) // 4), kind], kv.at[d, kind], at_y(d))
            links.add(("back", d, kind), contrib.at[d, kind], rkv.at[d - 1, kind], at_y(-d))
    for d in (1, 2, 3):
        cols = pl.ds(pl.multiple_of(first_col(lax.rem(z + d, 4)), 128), 1024)
        links.add(("hid", d), hid.at[half, cols], hz.at[d - 1, half], at_z(d))
        links.add(("hid_mate", d), hz.at[d - 1, half], hz.at[d - 1, half], mate)
        links.add(("x", d), term.at[0, d], r2.at[d - 1], at_x(d))
    for k in range(4):
        links.add(("core", k), term.at[1, k], r1.at[k], mate)
    spans = {"q": pl.ds(0, 2 * H), "k": pl.ds(2 * H, H), "v": pl.ds(3 * H, H)}
    for g, cols in spans.items():
        links.add(("dc", g, 1), dc.at[0, :, cols], dc.at[1, :, cols], at_z(1))
        links.add(("dc", g, 3), dc.at[0, :, cols], dc.at[3, :, cols], at_z(-1))
        links.add(("dc2", g, 1), dc.at[1, :128, cols], dc.at[2, :128, cols], at_z(1))
        links.add(("dc2", g, 3), dc.at[3, 128:, cols], dc.at[2, 128:, cols], at_z(-1))
    for g in range(4):
        links.add(("fwd", g, 1), part.at[2, g, :120], fwd.at[0, g], at_y(1))
        links.add(("fwd", g, 3), part.at[2, g, 120:], fwd.at[1, g], at_y(-1))
        links.add(("sum", g, 1), part.at[1, g], rpart.at[0, g], at_y(1))
        links.add(("sum", g, 3), part.at[3, g], rpart.at[1, g], at_y(-1))

    def columns(i):
        return pl.ds(pl.multiple_of(i * CH, CH), CH)

    def local_copy(j, i):
        if j == 0:
            return pltpu.make_async_copy(hid_h.at[:, columns(i)], hid.at[:, columns(i)], lsem.at[0, i])
        src, dst = ((wk_h, wk), (wv_h, wv), (wq_h, wq))[j - 1]
        return pltpu.make_async_copy(src.at[columns(i)], dst.at[columns(i)], lsem.at[j, i])

    for i in range(NCH):
        local_copy(0, i).start()
        local_copy(1, i).start()
    for j in (2, 3):
        for i in range(NCH):
            local_copy(j, i).start()
    grad_copy = pltpu.make_async_copy(grad_h, grad, lsem.at[4, 0])
    grad_copy.start()

    place = (s * T + lax.broadcasted_iota(jnp.int32, (T, H // 2), 0)).astype(F32)
    angle = place * freq_r[...]
    cos, sin = jnp.cos(angle), jnp.sin(angle)
    q_gain, k_gain = q_gain_r[...], k_gain_r[...]

    def project(j, weight, col, load_hid, load_w):
        def step(i, acc):
            if load_hid:
                local_copy(0, i).wait()
            if load_w:
                local_copy(j, i).wait()
            left = split(hid[:, columns(i)])
            right = split(weight[columns(i), col : col + H])
            return acc + product(left, right, NN)

        return lax.fori_loop(0, NCH, step, jnp.zeros((T, H), F32))

    def send_own(kind):
        links.start("kv", 4, kind)
        for d in (1, 2, 3):
            @pl.when(y + d < 4)
            def _():
                links.start("kv", d, kind)

    def send_prev(kind):
        links.arrived("kv", 4, kind)
        for d in (1, 2, 3):
            @pl.when(y + d >= 4)
            def _():
                links.start("kv", d, kind)

    key_raw = project(1, wk, 0, True, True)
    raw[2] = key_raw
    kv[0, 0] = rotate(key_raw * inv_rms(key_raw) * k_gain, cos, sin)
    pl.semaphore_wait(barrier, len(partners))
    send_own(0)
    kv[0, 1] = project(2, wv, 0, False, True)
    send_own(1)

    def query(h, load):
        q_raw = project(3, wq, h * H, False, load)
        raw[h] = q_raw
        q2[h * T : (h + 1) * T, :] = rotate(q_raw * inv_rms(q_raw) * q_gain, cos, sin) * (H ** -0.5)

    query(0, True)
    send_prev(0)
    query(1, False)
    send_prev(1)
    grad_copy.wait()

    for d in (1, 2, 3):
        links.start("hid", d)

    def q_pair():
        return split(q2[...])

    def g_pair():
        return split(jnp.concatenate([grad[:, :H], grad[:, H:]], axis=0))

    row = lax.broadcasted_iota(jnp.int32, (T, 2 * T), 0)
    col = lax.rem(lax.broadcasted_iota(jnp.int32, (T, 2 * T), 1), T)

    def segments(blk):
        return seg[:, pl.ds(pl.multiple_of(blk * T, T), T)]

    seg_q = segments(s)
    seg_q = jnp.concatenate([seg_q, seg_q], axis=1)

    def forward(d, total, delta):
        seg_k = jnp.broadcast_to(segments(lax.rem(s - d + 16, 16)), (T, T)).T
        seg_k = jnp.concatenate([seg_k, seg_k], axis=1)
        dist = 256 * d + col - row
        allowed = (dist >= 0) & (dist < WINDOW) & (seg_k == seg_q) & (s - d >= 0)
        scores = product(split(kv[d, 0]), q_pair(), NT)
        weights = jnp.where(allowed, jnp.exp(scores), 0.0)
        wt[d] = weights
        d_shares = product(split(kv[d, 1]), g_pair(), NT)
        dpt[d] = d_shares
        total = total + jnp.sum(weights, axis=0, keepdims=True)
        delta = delta + jnp.sum(weights * d_shares, axis=0, keepdims=True)
        return total, delta

    total = delta = jnp.zeros((1, 2 * T), F32)
    for d in (0, 4, 1, 3, 2):
        if d in (1, 2, 3):
            links.arrived("kv", d, 0)
            links.arrived("kv", d, 1)
        total, delta = forward(d, total, delta)
    inverse = 1.0 / total
    delta = delta * inverse

    def back_values(d):
        shares = wt[d] * inverse
        wt[d] = shares
        contrib[d, 1] = product(split(shares), g_pair(), NN)

    def back_keys(d, first):
        d_scores = split(wt[d] * (dpt[d] - delta))
        contrib[d, 0] = product(d_scores, q_pair(), NN)
        if d in (1, 2, 3):
            links.start("back", d, 0)
        more = product(split(kv[d, 0]), d_scores, TN)
        dqt[...] = more if first else dqt[...] + more

    for d in (2, 1, 3):
        back_values(d)
        links.start("back", d, 1)
    for d in (2, 1, 3):
        back_keys(d, d == 2)
    for d in (4, 0):
        back_values(d)
        back_keys(d, False)
    d_q = dqt[...].T * (H ** -0.5)
    for h in (0, 1):
        dc[0, :, h * H : (h + 1) * H] = norm_back(raw[h], q_gain, unrotate(d_q[h * T : (h + 1) * T], cos, sin))

    def spread(g):
        links.start("dc", g, 1)
        links.start("dc", g, 3)

    def spread_on(g):
        for d in (1, 3):
            links.arrived("dc", g, d)
            links.start("dc2", g, d)

    def gathered(g):
        for d in (1, 3):
            links.arrived("dc2", g, d)

    spread("q")

    out_t = None
    for d in range(5):
        more = product(split(kv[d, 1]), split(wt[d]), TN)
        out_t = more if out_t is None else out_t + more
    attended = out_t.T
    att_o[:, :H] = attended[:T]
    att_o[:, H:] = attended[T:]

    for d in (1, 2, 3):
        links.arrived("hid", d)
        links.start("hid_mate", d)

    def transpose_into(d, read):
        def step(i, carry):
            lanes = pl.multiple_of(i * 256, 256)
            high, low = split(read(lanes).T)
            ht_h[pl.ds(lanes, 256), d * T : (d + 1) * T] = high
            ht_l[pl.ds(lanes, 256), d * T : (d + 1) * T] = low
            return carry

        lax.fori_loop(0, 4, step, 0)

    base = first_col(z)
    transpose_into(0, lambda lanes: hid[:, pl.ds(pl.multiple_of(base + lanes, 128), 256)])
    for d in (1, 2, 3):
        links.arrived("hid_mate", d)
        transpose_into(d, lambda lanes: hz[d - 1, :, pl.ds(lanes, 256)])

    def collect(kind):
        mine, before = contrib[0, kind], contrib[4, kind]
        for d in (1, 2, 3):
            links.arrived("back", d, kind)
            got = rkv[d - 1, kind]
            inside = jnp.where(y + d < 4, 1.0, 0.0).astype(F32)
            mine = mine + inside * got
            before = before + (1.0 - inside) * got
        prev[kind] = before
        contrib[0, kind] = mine
        links.start("prev", kind)

    collect(1)
    spread_on("q")
    collect(0)

    off = lax.rem(z, 2) * 64

    def partial(g):
        pieces = [split(dc[k, :, g * H : (g + 1) * H]) for k in range(4)]
        right = tuple(jnp.concatenate([p[i] for p in pieces], axis=0) for i in (0, 1))
        for d in (2, 1, 3, 0):
            rows = pl.ds(pl.multiple_of(off + 240 * lax.rem(y + d, 4), 16), 240)
            part[d, g] = product((ht_h[rows, :], ht_l[rows, :]), right, NN)
            if d == 2:
                links.start("fwd", g, 1)
                links.start("fwd", g, 3)

    def pass_on(g):
        links.arrived("fwd", g, 1)
        part[1, g, :120] = part[1, g, :120] + fwd[0, g]
        links.start("sum", g, 1)
        links.arrived("fwd", g, 3)
        part[3, g, 120:] = part[3, g, 120:] + fwd[1, g]
        links.start("sum", g, 3)

    def summed(g):
        links.arrived("sum", g, 1)
        links.arrived("sum", g, 3)
        return part[0, g] + (rpart[0, g] + rpart[1, g])

    gathered("q")
    partial(0)
    partial(1)

    links.arrived("prev", 1)
    dc[0, :, 3 * H : 4 * H] = contrib[0, 1] + zr[1]
    spread("v")
    pass_on(0)
    pass_on(1)
    links.arrived("prev", 0)
    d_key = unrotate(contrib[0, 0] + zr[0], cos, sin)
    dc[0, :, 2 * H : 3 * H] = norm_back(raw[2], k_gain, d_key)
    spread("k")

    d_own = [split(dc[0, :, g * H : (g + 1) * H]) for g in range(4)]
    weights = [(wq, 0), (wq, H), (wk, 0), (wv, 0)]

    def input_term(tt):
        rows = pl.ds(pl.multiple_of(tt * 480, 32), 480)
        acc = None
        for g in range(4):
            w, first = weights[g]
            one = product(split(w[rows, first : first + H]), d_own[g], NT)
            acc = one if acc is None else acc + one
        return acc

    for k in (1, 2, 3, 0):
        term[1, k] = input_term(2 * lax.rem(x + k, 4) + 1 - c)
        links.start("core", k)
    spread_on("v")
    for k in (1, 2, 3, 0):
        mine = input_term(2 * lax.rem(x + k, 4) + c)
        links.arrived("core", k)
        term[0, k] = mine + r1[k]
        if k:
            links.start("x", k)
    spread_on("k")

    gathered("v")
    partial(3)
    gathered("k")
    partial(2)
    pass_on(3)
    pass_on(2)

    gq_o[:, :H] = summed(0)
    gq_o[:, H:] = summed(1)
    total_in = term[0, 0]
    for k in (1, 2, 3):
        links.arrived("x", k)
        total_in = total_in + r2[k - 1]
    gin_o[...] = total_in
    gv_o[...] = summed(3)
    gk_o[...] = summed(2)
    links.finish()


def hand_over(*refs):
    count = (len(refs) - 1) // 2
    copies = [pltpu.make_async_copy(refs[i], refs[count + i], refs[-1].at[i]) for i in range(count)]
    for copy in copies:
        copy.start()
    for copy in copies:
        copy.wait()


def local(hidden_in, query_proj, key_proj, value_proj, query_gain, key_gain, segment_ids, grad_out):
    frequency = np.power(10000.0, -2.0 * np.arange(H // 2) / H).astype(np.float32)[None, :]
    vmem = pl.BlockSpec(memory_space=pltpu.VMEM)
    hbm = pl.BlockSpec(memory_space=pl.ANY)
    V, S = pltpu.VMEM, pltpu.SemaphoreType.DMA
    shape = jax.ShapeDtypeStruct
    outs = (
        shape((T, 512), F32), shape((480, T), F32), shape((240, 512), F32), shape((240, 256), F32), shape((240, 256), F32),
    )
    results = pl.pallas_call(
        kernel,
        out_shape=outs,
        in_specs=[hbm] * 5 + [vmem] * 4,
        out_specs=(vmem,) * 5,
        scratch_shapes=[
            V((T, D), F32), V((D, 512), F32), V((D, 256), F32), V((D, 256), F32), V((T, 512), F32),
            V((3, T, H), F32), V((2 * T, H), F32), V((5, 2, T, H), F32), V((5, T, 2 * T), F32), V((5, T, 2 * T), F32),
            V((H, 2 * T), F32), V((5, 2, T, H), F32), V((3, 2, T, H), F32), V((2, T, H), F32), V((2, T, H), F32),
            V((3, T, 1024), F32), V((1024, 1024), BF16), V((1024, 1024), BF16), V((4, T, 1024), F32),
            V((4, 4, 240, H), F32), V((2, 4, 120, H), F32), V((2, 4, 240, H), F32),
            V((2, 4, 480, T), F32), V((4, 480, T), F32), V((3, 480, T), F32),
            S((5, NCH)), S((COPIES,)), S((COPIES,)),
        ],
        compiler_params=pltpu.CompilerParams(collective_id=0, has_side_effects=True, vmem_limit_bytes=63 << 20),
        cost_estimate=pl.CostEstimate(flops=24_000_000_000, bytes_accessed=40_000_000, transcendentals=700_000),
    )(
        hidden_in, query_proj, key_proj, value_proj, grad_out,
        query_gain.reshape(1, H), key_gain.reshape(1, H), segment_ids.reshape(1, -1), jnp.asarray(frequency),
    )
    attended, grad_in, grad_query, grad_key, grad_value = pl.pallas_call(
        hand_over, out_shape=outs, in_specs=[hbm] * 5, out_specs=(hbm,) * 5, scratch_shapes=[S((5,))],
    )(*results)
    return attended, grad_in.T, grad_query, grad_key, grad_value


def solution(mesh):
    return jax.shard_map(
        local,
        mesh=mesh,
        in_specs=(
            P("seq", None), P(None, "tensor"), P(None, "tensor"), P(None, "tensor"), P(), P(), P(), P("seq", "tensor"),
        ),
        out_specs=(P("seq", "tensor"),) * 5,
        check_vma=False,
    )
```

```python
import functools

import jax
import jax.numpy as jnp
import numpy as np
from jax import lax
from jax.experimental import pallas as pl
from jax.experimental.pallas import tpu as pltpu
from jax.sharding import PartitionSpec as P

MESH = pl.DeviceIdType.MESH
WINDOW = 1024
EPS = 1e-06
T = 256
H = 256
D = 3840
NCH = 5
CH = D // NCH
F32, BF16 = jnp.float32, jnp.bfloat16

NN = (((1,), (0,)), ((), ()))
NT = (((1,), (1,)), ((), ()))
TN = (((0,), (0,)), ((), ()))


def split(value):
    high = value.astype(BF16)
    return high, (value - high.astype(F32)).astype(BF16)


def product(left, right, dims):
    (lh, ll), (rh, rl) = left, right
    dot = functools.partial(lax.dot_general, dimension_numbers=dims, preferred_element_type=F32)
    return dot(lh, rh) + (dot(lh, rl) + dot(ll, rh))


def rotate(u, cos, sin):
    a, b = u[:, :128], u[:, 128:]
    return jnp.concatenate([a * cos - b * sin, b * cos + a * sin], axis=1)


def unrotate(u, cos, sin):
    a, b = u[:, :128], u[:, 128:]
    return jnp.concatenate([a * cos + b * sin, b * cos - a * sin], axis=1)


def inv_rms(x):
    return lax.rsqrt(jnp.mean(x * x, axis=1, keepdims=True) + EPS)


def norm_back(x, gain, d_norm):
    r = inv_rms(x)
    gd = d_norm * gain
    return r * gd - x * (r * r * r) * jnp.mean(x * gd, axis=1, keepdims=True)


class Links:
    def __init__(self, send_sems, recv_sems):
        self.sems = send_sems, recv_sems
        self.copies = {}

    def add(self, name, src, dst, device):
        i = len(self.copies)
        self.copies[name] = pltpu.make_async_remote_copy(
            src_ref=src, dst_ref=dst, send_sem=self.sems[0].at[i], recv_sem=self.sems[1].at[i],
            device_id=device, device_id_type=MESH,
        )

    def start(self, *name):
        self.copies[name].start()

    def arrived(self, *name):
        self.copies[name].wait_recv()

    def finish(self):
        for copy in self.copies.values():
            copy.wait_send()


COPIES = 64


def kernel(
    hid_h, wq_h, wk_h, wv_h, grad_h, q_gain_r, k_gain_r, seg, freq_r,
    att_o, gin_o, gq_o, gk_o, gv_o,
    hid, wq, wk, wv, grad, raw, q2, kv, wt, dpt, dqt, contrib, rkv, prev, zr,
    hz, ht_h, ht_l, dc, part, fwd, rpart, term, r1, r2, lsem, send_sems, recv_sems,
):
    s = lax.axis_index("seq")
    t = lax.axis_index("tensor")
    z, y = s // 4, lax.rem(s, 4)
    x, c = t // 2, lax.rem(t, 2)

    def at_z(d):
        return (lax.rem(z + d + 4, 4) * 4 + y, t)

    def at_y(d):
        return (z * 4 + lax.rem(y + d + 4, 4), t)

    def at_x(d):
        return (s, lax.rem(x + d + 4, 4) * 2 + c)

    mate = (s, x * 2 + 1 - c)
    barrier = pltpu.get_barrier_semaphore()
    partners = [at_z(1), at_z(2), at_z(3), at_y(1), at_y(2), at_y(3), at_x(1), at_x(2), at_x(3), mate]
    for dev in partners:
        pl.semaphore_signal(barrier, inc=1, device_id=dev, device_id_type=MESH)

    links = Links(send_sems, recv_sems)
    half = pl.ds(pl.multiple_of(c * 128, 128), 128)

    def first_col(zz):
        return ((15 * zz) // 2) * 128

    for kind in (0, 1):
        links.add(("kv", 4, kind), kv.at[0, kind], kv.at[4, kind], at_z(1))
        links.add(("prev", kind), prev.at[kind], zr.at[kind], at_z(-1))
        for d in (1, 2, 3):
            links.add(("kv", d, kind), kv.at[4 * ((y + d) // 4), kind], kv.at[d, kind], at_y(d))
            links.add(("back", d, kind), contrib.at[d, kind], rkv.at[d - 1, kind], at_y(-d))
    for d in (1, 2, 3):
        cols = pl.ds(pl.multiple_of(first_col(lax.rem(z + d, 4)), 128), 1024)
        links.add(("hid", d), hid.at[half, cols], hz.at[d - 1, half], at_z(d))
        links.add(("hid_mate", d), hz.at[d - 1, half], hz.at[d - 1, half], mate)
        links.add(("x", d), term.at[0, d], r2.at[d - 1], at_x(d))
    for k in range(4):
        links.add(("core", k), term.at[1, k], r1.at[k], mate)
    spans = {"q": pl.ds(0, 2 * H), "k": pl.ds(2 * H, H), "v": pl.ds(3 * H, H)}
    for g, cols in spans.items():
        links.add(("dc", g, 1), dc.at[0, :, cols], dc.at[1, :, cols], at_z(1))
        links.add(("dc", g, 3), dc.at[0, :, cols], dc.at[3, :, cols], at_z(-1))
        links.add(("dc2", g, 1), dc.at[1, :128, cols], dc.at[2, :128, cols], at_z(1))
        links.add(("dc2", g, 3), dc.at[3, 128:, cols], dc.at[2, 128:, cols], at_z(-1))
    for g in range(4):
        links.add(("fwd", g, 1), part.at[2, g, :120], fwd.at[0, g], at_y(1))
        links.add(("fwd", g, 3), part.at[2, g, 120:], fwd.at[1, g], at_y(-1))
        links.add(("sum", g, 1), part.at[1, g], rpart.at[0, g], at_y(1))
        links.add(("sum", g, 3), part.at[3, g], rpart.at[1, g], at_y(-1))

    def columns(i):
        return pl.ds(pl.multiple_of(i * CH, CH), CH)

    def local_copy(j, i):
        if j == 0:
            return pltpu.make_async_copy(hid_h.at[:, columns(i)], hid.at[:, columns(i)], lsem.at[0, i])
        src, dst = ((wk_h, wk), (wv_h, wv), (wq_h, wq))[j - 1]
        return pltpu.make_async_copy(src.at[columns(i)], dst.at[columns(i)], lsem.at[j, i])

    for i in range(NCH):
        local_copy(0, i).start()
        local_copy(1, i).start()
    for j in (2, 3):
        for i in range(NCH):
            local_copy(j, i).start()
    grad_copy = pltpu.make_async_copy(grad_h, grad, lsem.at[4, 0])
    grad_copy.start()

    place = (s * T + lax.broadcasted_iota(jnp.int32, (T, H // 2), 0)).astype(F32)
    angle = place * freq_r[...]
    cos, sin = jnp.cos(angle), jnp.sin(angle)
    q_gain, k_gain = q_gain_r[...], k_gain_r[...]

    def project(j, weight, col, load_hid, load_w):
        def step(i, acc):
            if load_hid:
                local_copy(0, i).wait()
            if load_w:
                local_copy(j, i).wait()
            left = split(hid[:, columns(i)])
            right = split(weight[columns(i), col : col + H])
            return acc + product(left, right, NN)

        return lax.fori_loop(0, NCH, step, jnp.zeros((T, H), F32))

    def send_own(kind):
        links.start("kv", 4, kind)
        for d in (1, 2, 3):
            @pl.when(y + d < 4)
            def _():
                links.start("kv", d, kind)

    def send_prev(kind):
        links.arrived("kv", 4, kind)
        for d in (1, 2, 3):
            @pl.when(y + d >= 4)
            def _():
                links.start("kv", d, kind)

    key_raw = project(1, wk, 0, True, True)
    raw[2] = key_raw
    kv[0, 0] = rotate(key_raw * inv_rms(key_raw) * k_gain, cos, sin)
    pl.semaphore_wait(barrier, len(partners))
    send_own(0)
    kv[0, 1] = project(2, wv, 0, False, True)
    send_own(1)

    def query(h, load):
        q_raw = project(3, wq, h * H, False, load)
        raw[h] = q_raw
        q2[h * T : (h + 1) * T, :] = rotate(q_raw * inv_rms(q_raw) * q_gain, cos, sin) * (H ** -0.5)

    query(0, True)
    send_prev(0)
    query(1, False)
    send_prev(1)
    grad_copy.wait()

    for d in (1, 2, 3):
        links.start("hid", d)

    def q_pair():
        return split(q2[...])

    def g_pair():
        return split(jnp.concatenate([grad[:, :H], grad[:, H:]], axis=0))

    row = lax.broadcasted_iota(jnp.int32, (T, 2 * T), 0)
    col = lax.rem(lax.broadcasted_iota(jnp.int32, (T, 2 * T), 1), T)

    def segments(blk):
        return seg[:, pl.ds(pl.multiple_of(blk * T, T), T)]

    seg_q = segments(s)
    seg_q = jnp.concatenate([seg_q, seg_q], axis=1)

    def forward(d, total, delta):
        seg_k = jnp.broadcast_to(segments(lax.rem(s - d + 16, 16)), (T, T)).T
        seg_k = jnp.concatenate([seg_k, seg_k], axis=1)
        dist = 256 * d + col - row
        allowed = (dist >= 0) & (dist < WINDOW) & (seg_k == seg_q) & (s - d >= 0)
        scores = product(split(kv[d, 0]), q_pair(), NT)
        weights = jnp.where(allowed, jnp.exp(scores), 0.0)
        wt[d] = weights
        d_shares = product(split(kv[d, 1]), g_pair(), NT)
        dpt[d] = d_shares
        total = total + jnp.sum(weights, axis=0, keepdims=True)
        delta = delta + jnp.sum(weights * d_shares, axis=0, keepdims=True)
        return total, delta

    total = delta = jnp.zeros((1, 2 * T), F32)
    for d in (0, 4, 1, 3, 2):
        if d in (1, 2, 3):
            links.arrived("kv", d, 0)
            links.arrived("kv", d, 1)
        total, delta = forward(d, total, delta)
    inverse = 1.0 / total
    delta = delta * inverse

    def back_values(d):
        shares = wt[d] * inverse
        wt[d] = shares
        contrib[d, 1] = product(split(shares), g_pair(), NN)

    def back_keys(d, first):
        d_scores = split(wt[d] * (dpt[d] - delta))
        contrib[d, 0] = product(d_scores, q_pair(), NN)
        if d in (1, 2, 3):
            links.start("back", d, 0)
        more = product(split(kv[d, 0]), d_scores, TN)
        dqt[...] = more if first else dqt[...] + more

    for d in (2, 1, 3):
        back_values(d)
        links.start("back", d, 1)
    for d in (2, 1, 3):
        back_keys(d, d == 2)
    for d in (4, 0):
        back_values(d)
        back_keys(d, False)
    d_q = dqt[...].T * (H ** -0.5)
    for h in (0, 1):
        dc[0, :, h * H : (h + 1) * H] = norm_back(raw[h], q_gain, unrotate(d_q[h * T : (h + 1) * T], cos, sin))

    def spread(g):
        links.start("dc", g, 1)
        links.start("dc", g, 3)

    def spread_on(g):
        for d in (1, 3):
            links.arrived("dc", g, d)
            links.start("dc2", g, d)

    def gathered(g):
        for d in (1, 3):
            links.arrived("dc2", g, d)

    spread("q")

    out_t = None
    for d in range(5):
        more = product(split(kv[d, 1]), split(wt[d]), TN)
        out_t = more if out_t is None else out_t + more
    attended = out_t.T
    att_o[:, :H] = attended[:T]
    att_o[:, H:] = attended[T:]

    for d in (1, 2, 3):
        links.arrived("hid", d)
        links.start("hid_mate", d)

    def transpose_into(d, read):
        def step(i, carry):
            lanes = pl.multiple_of(i * 256, 256)
            high, low = split(read(lanes).T)
            ht_h[pl.ds(lanes, 256), d * T : (d + 1) * T] = high
            ht_l[pl.ds(lanes, 256), d * T : (d + 1) * T] = low
            return carry

        lax.fori_loop(0, 4, step, 0)

    base = first_col(z)
    transpose_into(0, lambda lanes: hid[:, pl.ds(pl.multiple_of(base + lanes, 128), 256)])
    for d in (1, 2, 3):
        links.arrived("hid_mate", d)
        transpose_into(d, lambda lanes: hz[d - 1, :, pl.ds(lanes, 256)])

    def collect(kind):
        mine, before = contrib[0, kind], contrib[4, kind]
        for d in (1, 2, 3):
            links.arrived("back", d, kind)
            got = rkv[d - 1, kind]
            inside = jnp.where(y + d < 4, 1.0, 0.0).astype(F32)
            mine = mine + inside * got
            before = before + (1.0 - inside) * got
        prev[kind] = before
        contrib[0, kind] = mine
        links.start("prev", kind)

    collect(1)
    spread_on("q")
    collect(0)

    off = lax.rem(z, 2) * 64

    def partial(g):
        pieces = [split(dc[k, :, g * H : (g + 1) * H]) for k in range(4)]
        right = tuple(jnp.concatenate([p[i] for p in pieces], axis=0) for i in (0, 1))
        for d in (2, 1, 3, 0):
            rows = pl.ds(pl.multiple_of(off + 240 * lax.rem(y + d, 4), 16), 240)
            part[d, g] = product((ht_h[rows, :], ht_l[rows, :]), right, NN)
            if d == 2:
                links.start("fwd", g, 1)
                links.start("fwd", g, 3)

    def pass_on(g):
        links.arrived("fwd", g, 1)
        part[1, g, :120] = part[1, g, :120] + fwd[0, g]
        links.start("sum", g, 1)
        links.arrived("fwd", g, 3)
        part[3, g, 120:] = part[3, g, 120:] + fwd[1, g]
        links.start("sum", g, 3)

    def summed(g):
        links.arrived("sum", g, 1)
        links.arrived("sum", g, 3)
        return part[0, g] + (rpart[0, g] + rpart[1, g])

    gathered("q")
    partial(0)
    partial(1)

    links.arrived("prev", 1)
    dc[0, :, 3 * H : 4 * H] = contrib[0, 1] + zr[1]
    spread("v")
    pass_on(0)
    pass_on(1)
    links.arrived("prev", 0)
    d_key = unrotate(contrib[0, 0] + zr[0], cos, sin)
    dc[0, :, 2 * H : 3 * H] = norm_back(raw[2], k_gain, d_key)
    spread("k")

    d_own = [split(dc[0, :, g * H : (g + 1) * H]) for g in range(4)]
    weights = [(wq, 0), (wq, H), (wk, 0), (wv, 0)]

    def input_term(tt):
        rows = pl.ds(pl.multiple_of(tt * 480, 32), 480)
        acc = None
        for g in range(4):
            w, first = weights[g]
            one = product(split(w[rows, first : first + H]), d_own[g], NT)
            acc = one if acc is None else acc + one
        return acc

    for k in (1, 2, 3, 0):
        term[1, k] = input_term(2 * lax.rem(x + k, 4) + 1 - c)
        links.start("core", k)
    spread_on("v")
    for k in (1, 2, 3, 0):
        mine = input_term(2 * lax.rem(x + k, 4) + c)
        links.arrived("core", k)
        term[0, k] = mine + r1[k]
        if k:
            links.start("x", k)
    spread_on("k")

    gathered("v")
    partial(3)
    gathered("k")
    partial(2)
    pass_on(3)
    pass_on(2)

    gq_o[:, :H] = summed(0)
    gq_o[:, H:] = summed(1)
    total_in = term[0, 0]
    for k in (1, 2, 3):
        links.arrived("x", k)
        total_in = total_in + r2[k - 1]
    gin_o[...] = total_in
    gv_o[...] = summed(3)
    gk_o[...] = summed(2)
    links.finish()


def hand_over(*refs):
    ins, outs, held, sems = refs[:5], refs[5:10], refs[10:15], refs[15]
    loads = [pltpu.make_async_copy(ins[i], held[i], sems.at[0, i]) for i in range(5)]
    stores = [pltpu.make_async_copy(held[i], outs[i], sems.at[1, i]) for i in range(5)]
    for load in loads:
        load.start()
    for load, store in zip(loads, stores):
        load.wait()
        store.start()
    for store in stores:
        store.wait()


def local(hidden_in, query_proj, key_proj, value_proj, query_gain, key_gain, segment_ids, grad_out):
    frequency = np.power(10000.0, -2.0 * np.arange(H // 2) / H).astype(np.float32)[None, :]
    vmem = pl.BlockSpec(memory_space=pltpu.VMEM)
    hbm = pl.BlockSpec(memory_space=pl.ANY)
    V, S = pltpu.VMEM, pltpu.SemaphoreType.DMA
    shape = jax.ShapeDtypeStruct
    outs = (
        shape((T, 512), F32), shape((480, T), F32), shape((240, 512), F32), shape((240, 256), F32), shape((240, 256), F32),
    )
    results = pl.pallas_call(
        kernel,
        out_shape=outs,
        in_specs=[hbm] * 5 + [vmem] * 4,
        out_specs=(vmem,) * 5,
        scratch_shapes=[
            V((T, D), F32), V((D, 512), F32), V((D, 256), F32), V((D, 256), F32), V((T, 512), F32),
            V((3, T, H), F32), V((2 * T, H), F32), V((5, 2, T, H), F32), V((5, T, 2 * T), F32), V((5, T, 2 * T), F32),
            V((H, 2 * T), F32), V((5, 2, T, H), F32), V((3, 2, T, H), F32), V((2, T, H), F32), V((2, T, H), F32),
            V((3, T, 1024), F32), V((1024, 1024), BF16), V((1024, 1024), BF16), V((4, T, 1024), F32),
            V((4, 4, 240, H), F32), V((2, 4, 120, H), F32), V((2, 4, 240, H), F32),
            V((2, 4, 480, T), F32), V((4, 480, T), F32), V((3, 480, T), F32),
            S((5, NCH)), S((COPIES,)), S((COPIES,)),
        ],
        compiler_params=pltpu.CompilerParams(collective_id=0, has_side_effects=True, vmem_limit_bytes=63 << 20),
        cost_estimate=pl.CostEstimate(flops=24_000_000_000, bytes_accessed=40_000_000, transcendentals=700_000),
    )(
        hidden_in, query_proj, key_proj, value_proj, grad_out,
        query_gain.reshape(1, H), key_gain.reshape(1, H), segment_ids.reshape(1, -1), jnp.asarray(frequency),
    )
    attended, grad_in, grad_query, grad_key, grad_value = pl.pallas_call(
        hand_over, out_shape=outs, in_specs=[hbm] * 5, out_specs=(hbm,) * 5,
        scratch_shapes=[V(out.shape, F32) for out in outs] + [S((2, 5))],
    )(*results)
    return attended, grad_in.T, grad_query, grad_key, grad_value


def solution(mesh):
    return jax.shard_map(
        local,
        mesh=mesh,
        in_specs=(
            P("seq", None), P(None, "tensor"), P(None, "tensor"), P(None, "tensor"), P(), P(), P(), P("seq", "tensor"),
        ),
        out_specs=(P("seq", "tensor"),) * 5,
        check_vma=False,
    )
```

```python
import functools

import jax
import jax.numpy as jnp
import numpy as np
from jax import lax
from jax.experimental import pallas as pl
from jax.experimental.pallas import tpu as pltpu
from jax.sharding import PartitionSpec as P

MESH = pl.DeviceIdType.MESH
WINDOW = 1024
EPS = 1e-06
T = 256
H = 256
D = 3840
NCH = 5
CH = D // NCH
F32, BF16 = jnp.float32, jnp.bfloat16

NN = (((1,), (0,)), ((), ()))
NT = (((1,), (1,)), ((), ()))
TN = (((0,), (0,)), ((), ()))


def split(value):
    high = value.astype(BF16)
    return high, (value - high.astype(F32)).astype(BF16)


def product(left, right, dims):
    (lh, ll), (rh, rl) = left, right
    dot = functools.partial(lax.dot_general, dimension_numbers=dims, preferred_element_type=F32)
    return dot(lh, rh) + (dot(lh, rl) + dot(ll, rh))


def rotate(u, cos, sin):
    a, b = u[:, :128], u[:, 128:]
    return jnp.concatenate([a * cos - b * sin, b * cos + a * sin], axis=1)


def unrotate(u, cos, sin):
    a, b = u[:, :128], u[:, 128:]
    return jnp.concatenate([a * cos + b * sin, b * cos - a * sin], axis=1)


def inv_rms(x):
    return lax.rsqrt(jnp.mean(x * x, axis=1, keepdims=True) + EPS)


def norm_back(x, gain, d_norm):
    r = inv_rms(x)
    gd = d_norm * gain
    return r * gd - x * (r * r * r) * jnp.mean(x * gd, axis=1, keepdims=True)


class Links:
    def __init__(self, send_sems, recv_sems):
        self.sems = send_sems, recv_sems
        self.copies = {}

    def add(self, name, src, dst, device):
        i = len(self.copies)
        self.copies[name] = pltpu.make_async_remote_copy(
            src_ref=src, dst_ref=dst, send_sem=self.sems[0].at[i], recv_sem=self.sems[1].at[i],
            device_id=device, device_id_type=MESH,
        )

    def start(self, *name):
        self.copies[name].start()

    def arrived(self, *name):
        self.copies[name].wait_recv()

    def finish(self):
        for copy in self.copies.values():
            copy.wait_send()


COPIES = 64


def kernel(
    hid_h, wq_h, wk_h, wv_h, grad_h, q_gain_r, k_gain_r, seg, freq_r,
    att_o, gin_o, gq_o, gk_o, gv_o,
    hid, wq, wk, wv, grad, raw, q2, kv, wt, dpt, dqt, contrib, rkv, prev, zr,
    hz, ht_h, ht_l, dc, part, fwd, rpart, term, r1, r2, xfwd, lsem, osem, send_sems, recv_sems,
):
    s = lax.axis_index("seq")
    t = lax.axis_index("tensor")
    z, y = s // 4, lax.rem(s, 4)
    x, c = t // 2, lax.rem(t, 2)

    def at_z(d):
        return (lax.rem(z + d + 4, 4) * 4 + y, t)

    def at_y(d):
        return (z * 4 + lax.rem(y + d + 4, 4), t)

    def at_x(d):
        return (s, lax.rem(x + d + 4, 4) * 2 + c)

    mate = (s, x * 2 + 1 - c)
    barrier = pltpu.get_barrier_semaphore()
    partners = [at_z(1), at_z(2), at_z(3), at_y(1), at_y(2), at_y(3), at_x(1), at_x(2), at_x(3), mate]
    for dev in partners:
        pl.semaphore_signal(barrier, inc=1, device_id=dev, device_id_type=MESH)

    links = Links(send_sems, recv_sems)
    half = pl.ds(pl.multiple_of(c * 128, 128), 128)

    def first_col(zz):
        return ((15 * zz) // 2) * 128

    pieces_of = {0: (pl.ds(0, 128), pl.ds(128, 128)), 1: (pl.ds(0, T),)}
    for kind in (0, 1):
        for i, rows in enumerate(pieces_of[kind]):
            links.add(("kv", 4, kind, i), kv.at[0, kind, rows], kv.at[4, kind, rows], at_z(1))
            for d in (1, 2, 3):
                src = kv.at[4 * ((y + d) // 4), kind, rows]
                links.add(("kv", d, kind, i), src, kv.at[d, kind, rows], at_y(d))
        links.add(("prev", kind), prev.at[kind], zr.at[kind], at_z(-1))
        for d in (1, 2, 3):
            links.add(("back", d, kind), contrib.at[d, kind], rkv.at[d - 1, kind], at_y(-d))
    for d in (1, 2, 3):
        cols = pl.ds(pl.multiple_of(first_col(lax.rem(z + d, 4)), 128), 1024)
        links.add(("hid", d), hid.at[half, cols], hz.at[d - 1, half], at_z(d))
        links.add(("hid_mate", d), hz.at[d - 1, half], hz.at[d - 1, half], mate)
    for k in range(4):
        links.add(("core", k), term.at[1, k], r1.at[k], mate)
    for i, d in enumerate((1, 3)):
        rows = pl.ds(240 * i, 240)
        links.add(("x_fwd", d), term.at[0, 2, rows], xfwd.at[i], at_x(d))
        links.add(("x", d), term.at[0, d], r2.at[i], at_x(d))
    spans = {"q": pl.ds(0, 2 * H), "k": pl.ds(2 * H, H), "v": pl.ds(3 * H, H)}
    for g, cols in spans.items():
        links.add(("dc", g, 1), dc.at[0, :, cols], dc.at[1, :, cols], at_z(1))
        links.add(("dc", g, 3), dc.at[0, :, cols], dc.at[3, :, cols], at_z(-1))
        links.add(("dc2", g, 1), dc.at[1, :128, cols], dc.at[2, :128, cols], at_z(1))
        links.add(("dc2", g, 3), dc.at[3, 128:, cols], dc.at[2, 128:, cols], at_z(-1))
    for g in range(4):
        links.add(("fwd", g, 1), part.at[2, g, :120], fwd.at[0, g], at_y(1))
        links.add(("fwd", g, 3), part.at[2, g, 120:], fwd.at[1, g], at_y(-1))
        links.add(("sum", g, 1), part.at[1, g], rpart.at[0, g], at_y(1))
        links.add(("sum", g, 3), part.at[3, g], rpart.at[1, g], at_y(-1))

    writes = []

    def write(i, src, dst):
        copy = pltpu.make_async_copy(src, dst, osem.at[i])
        copy.start()
        writes.append(copy)

    def columns(i):
        return pl.ds(pl.multiple_of(i * CH, CH), CH)

    def local_copy(j, i):
        if j == 0:
            return pltpu.make_async_copy(hid_h.at[:, columns(i)], hid.at[:, columns(i)], lsem.at[0, i])
        src, dst = ((wk_h, wk), (wv_h, wv), (wq_h, wq))[j - 1]
        return pltpu.make_async_copy(src.at[columns(i)], dst.at[columns(i)], lsem.at[j, i])

    for i in range(NCH):
        local_copy(0, i).start()
        local_copy(1, i).start()
    for j in (2, 3):
        for i in range(NCH):
            local_copy(j, i).start()
    grad_copy = pltpu.make_async_copy(grad_h, grad, lsem.at[4, 0])
    grad_copy.start()

    place = (s * T + lax.broadcasted_iota(jnp.int32, (T, H // 2), 0)).astype(F32)
    angle = place * freq_r[...]
    cos, sin = jnp.cos(angle), jnp.sin(angle)
    q_gain, k_gain = q_gain_r[...], k_gain_r[...]

    def project(j, weight, col, load_hid, load_w):
        def step(i, acc):
            if load_hid:
                local_copy(0, i).wait()
            if load_w:
                local_copy(j, i).wait()
            left = split(hid[:, columns(i)])
            right = split(weight[columns(i), col : col + H])
            return acc + product(left, right, NN)

        return lax.fori_loop(0, NCH, step, jnp.zeros((T, H), F32))

    def send_own(kind):
        for i in range(len(pieces_of[kind])):
            links.start("kv", 4, kind, i)
        for d in (1, 2, 3):
            @pl.when(y + d < 4)
            def _():
                for i in range(len(pieces_of[kind])):
                    links.start("kv", d, kind, i)

    def send_prev(kind):
        for i in range(len(pieces_of[kind])):
            links.arrived("kv", 4, kind, i)
            for d in (1, 2, 3):
                @pl.when(y + d >= 4)
                def _():
                    links.start("kv", d, kind, i)

    def have(d, kind):
        if d in (1, 2, 3):
            for i in range(len(pieces_of[kind])):
                links.arrived("kv", d, kind, i)

    key_raw = project(1, wk, 0, True, True)
    raw[2] = key_raw
    kv[0, 0] = rotate(key_raw * inv_rms(key_raw) * k_gain, cos, sin)
    pl.semaphore_wait(barrier, len(partners))
    send_own(0)
    kv[0, 1] = project(2, wv, 0, False, True)
    send_own(1)

    def query(h, load):
        q_raw = project(3, wq, h * H, False, load)
        raw[h] = q_raw
        q2[h * T : (h + 1) * T, :] = rotate(q_raw * inv_rms(q_raw) * q_gain, cos, sin) * (H ** -0.5)

    query(0, True)
    send_prev(0)
    query(1, False)
    send_prev(1)
    grad_copy.wait()

    for d in (1, 2, 3):
        links.start("hid", d)

    def q_pair():
        return split(q2[...])

    def g_pair():
        return split(jnp.concatenate([grad[:, :H], grad[:, H:]], axis=0))

    row = lax.broadcasted_iota(jnp.int32, (T, 2 * T), 0)
    col = lax.rem(lax.broadcasted_iota(jnp.int32, (T, 2 * T), 1), T)

    def segments(blk):
        return seg[:, pl.ds(pl.multiple_of(blk * T, T), T)]

    seg_q = segments(s)
    seg_q = jnp.concatenate([seg_q, seg_q], axis=1)

    def weigh(d):
        seg_k = jnp.broadcast_to(segments(lax.rem(s - d + 16, 16)), (T, T)).T
        seg_k = jnp.concatenate([seg_k, seg_k], axis=1)
        dist = 256 * d + col - row
        allowed = (dist >= 0) & (dist < WINDOW) & (seg_k == seg_q) & (s - d >= 0)
        scores = product(split(kv[d, 0]), q_pair(), NT)
        weights = jnp.where(allowed, jnp.exp(scores), 0.0)
        wt[d] = weights
        return jnp.sum(weights, axis=0, keepdims=True)

    def weigh_values(d):
        d_shares = product(split(kv[d, 1]), g_pair(), NT)
        dpt[d] = d_shares
        return jnp.sum(wt[d] * d_shares, axis=0, keepdims=True)

    total = delta = jnp.zeros((1, 2 * T), F32)
    for d in (0, 4):
        total = total + weigh(d)
    for d in (1, 3, 2):
        have(d, 0)
        total = total + weigh(d)
    inverse = 1.0 / total

    def back_values(d):
        shares = wt[d] * inverse
        wt[d] = shares
        contrib[d, 1] = product(split(shares), g_pair(), NN)

    def back_keys(d, first):
        d_scores = split(wt[d] * (dpt[d] - delta))
        contrib[d, 0] = product(d_scores, q_pair(), NN)
        if d in (1, 2, 3):
            links.start("back", d, 0)
        more = product(split(kv[d, 0]), d_scores, TN)
        dqt[...] = more if first else dqt[...] + more

    for d in (2, 1, 3):
        back_values(d)
        links.start("back", d, 1)
    for d in (4, 0):
        back_values(d)
        delta = delta + weigh_values(d)
    for d in (1, 3, 2):
        have(d, 1)
        delta = delta + weigh_values(d)
    for d in (2, 1, 3, 4, 0):
        back_keys(d, d == 2)
    d_q = dqt[...].T * (H ** -0.5)
    for h in (0, 1):
        dc[0, :, h * H : (h + 1) * H] = norm_back(raw[h], q_gain, unrotate(d_q[h * T : (h + 1) * T], cos, sin))

    def spread(g):
        links.start("dc", g, 1)
        links.start("dc", g, 3)

    def spread_on(g):
        for d in (1, 3):
            links.arrived("dc", g, d)
            links.start("dc2", g, d)

    def gathered(g):
        for d in (1, 3):
            links.arrived("dc2", g, d)

    spread("q")

    out_t = None
    for d in range(5):
        more = product(split(kv[d, 1]), split(wt[d]), TN)
        out_t = more if out_t is None else out_t + more
    q2[...] = out_t.T
    for h in (0, 1):
        write(h, q2.at[h * T : (h + 1) * T], att_o.at[:, h * H : (h + 1) * H])

    for d in (1, 2, 3):
        links.arrived("hid", d)
        links.start("hid_mate", d)

    def transpose_into(d, read):
        def step(i, carry):
            lanes = pl.multiple_of(i * 256, 256)
            high, low = split(read(lanes).T)
            ht_h[pl.ds(lanes, 256), d * T : (d + 1) * T] = high
            ht_l[pl.ds(lanes, 256), d * T : (d + 1) * T] = low
            return carry

        lax.fori_loop(0, 4, step, 0)

    base = first_col(z)
    transpose_into(0, lambda lanes: hid[:, pl.ds(pl.multiple_of(base + lanes, 128), 256)])
    for d in (1, 2, 3):
        links.arrived("hid_mate", d)
        transpose_into(d, lambda lanes: hz[d - 1, :, pl.ds(lanes, 256)])

    weights = [(wq, 0), (wq, H), (wk, 0), (wv, 0)]

    def input_part(k, core, grads):
        rows = pl.ds(pl.multiple_of((2 * lax.rem(x + k, 4) + core) * 480, 32), 480)
        acc = None
        for g, grad_g in grads.items():
            w, first = weights[g]
            one = product(split(w[rows, first : first + H]), grad_g, NT)
            acc = one if acc is None else acc + one
        return acc

    q_own = {g: split(dc[0, :, g * H : (g + 1) * H]) for g in (0, 1)}
    for k in range(4):
        term[0, k] = input_part(k, c, q_own)
        term[1, k] = input_part(k, 1 - c, q_own)

    def collect(kind):
        mine, before = contrib[0, kind], contrib[4, kind]
        for d in (1, 2, 3):
            links.arrived("back", d, kind)
            got = rkv[d - 1, kind]
            inside = jnp.where(y + d < 4, 1.0, 0.0).astype(F32)
            mine = mine + inside * got
            before = before + (1.0 - inside) * got
        prev[kind] = before
        contrib[0, kind] = mine
        links.start("prev", kind)

    collect(1)
    spread_on("q")
    collect(0)

    off = lax.rem(z, 2) * 64

    def partial(g):
        pieces = [split(dc[k, :, g * H : (g + 1) * H]) for k in range(4)]
        right = tuple(jnp.concatenate([p[i] for p in pieces], axis=0) for i in (0, 1))
        for d in (2, 1, 3, 0):
            rows = pl.ds(pl.multiple_of(off + 240 * lax.rem(y + d, 4), 16), 240)
            part[d, g] = product((ht_h[rows, :], ht_l[rows, :]), right, NN)
            if d == 2:
                links.start("fwd", g, 1)
                links.start("fwd", g, 3)

    def pass_on(g):
        links.arrived("fwd", g, 1)
        part[1, g, :120] = part[1, g, :120] + fwd[0, g]
        links.start("sum", g, 1)
        links.arrived("fwd", g, 3)
        part[3, g, 120:] = part[3, g, 120:] + fwd[1, g]
        links.start("sum", g, 3)

    def summed(g):
        links.arrived("sum", g, 1)
        links.arrived("sum", g, 3)
        part[0, g] = part[0, g] + (rpart[0, g] + rpart[1, g])
        dst = (gq_o.at[:, :H], gq_o.at[:, H:], gk_o, gv_o)[g]
        write(2 + g, part.at[0, g], dst)

    gathered("q")
    partial(0)
    partial(1)

    links.arrived("prev", 1)
    dc[0, :, 3 * H : 4 * H] = contrib[0, 1] + zr[1]
    spread("v")
    links.arrived("prev", 0)
    d_key = unrotate(contrib[0, 0] + zr[0], cos, sin)
    dc[0, :, 2 * H : 3 * H] = norm_back(raw[2], k_gain, d_key)
    spread("k")
    pass_on(0)
    pass_on(1)

    kv_own = {g: split(dc[0, :, g * H : (g + 1) * H]) for g in (2, 3)}

    def other(k):
        term[1, k] = term[1, k] + input_part(k, 1 - c, kv_own)
        links.start("core", k)

    def both(k):
        mine = term[0, k] + input_part(k, c, kv_own)
        links.arrived("core", k)
        term[0, k] = mine + r1[k]

    other(2)
    other(1)
    both(2)
    for d in (1, 3):
        links.start("x_fwd", d)
    spread_on("v")
    other(3)
    other(0)
    for k in (1, 3, 0):
        both(k)

    gathered("v")
    partial(3)
    spread_on("k")
    for i, d in enumerate((1, 3)):
        links.arrived("x_fwd", d)
        rows = pl.ds(240 * i, 240)
        term[0, d, rows] = term[0, d, rows] + xfwd[i]
        links.start("x", d)
    gathered("k")
    partial(2)
    pass_on(3)
    pass_on(2)

    summed(0)
    summed(1)
    links.arrived("x", 1)
    links.arrived("x", 3)
    term[0, 0] = term[0, 0] + (r2[0] + r2[1])
    write(6, term.at[0, 0], gin_o)
    summed(3)
    summed(2)
    for copy in writes:
        copy.wait()
    links.finish()


def hand_over(*refs):
    ins, outs, held, sems = refs[:5], refs[5:10], refs[10:15], refs[15]
    loads = [pltpu.make_async_copy(ins[i], held[i], sems.at[0, i]) for i in range(5)]
    stores = [pltpu.make_async_copy(held[i], outs[i], sems.at[1, i]) for i in range(5)]
    for load in loads:
        load.start()
    for load, store in zip(loads, stores):
        load.wait()
        store.start()
    for store in stores:
        store.wait()


def local(hidden_in, query_proj, key_proj, value_proj, query_gain, key_gain, segment_ids, grad_out):
    frequency = np.power(10000.0, -2.0 * np.arange(H // 2) / H).astype(np.float32)[None, :]
    vmem = pl.BlockSpec(memory_space=pltpu.VMEM)
    hbm = pl.BlockSpec(memory_space=pl.ANY)
    V, S = pltpu.VMEM, pltpu.SemaphoreType.DMA
    shape = jax.ShapeDtypeStruct
    outs = (
        shape((T, 512), F32), shape((480, T), F32), shape((240, 512), F32), shape((240, 256), F32), shape((240, 256), F32),
    )
    results = pl.pallas_call(
        kernel,
        out_shape=outs,
        in_specs=[hbm] * 5 + [vmem] * 4,
        out_specs=(hbm,) * 5,
        scratch_shapes=[
            V((T, D), F32), V((D, 512), F32), V((D, 256), F32), V((D, 256), F32), V((T, 512), F32),
            V((3, T, H), F32), V((2 * T, H), F32), V((5, 2, T, H), F32), V((5, T, 2 * T), F32), V((5, T, 2 * T), F32),
            V((H, 2 * T), F32), V((5, 2, T, H), F32), V((3, 2, T, H), F32), V((2, T, H), F32), V((2, T, H), F32),
            V((3, T, 1024), F32), V((1024, 1024), BF16), V((1024, 1024), BF16), V((4, T, 1024), F32),
            V((4, 4, 240, H), F32), V((2, 4, 120, H), F32), V((2, 4, 240, H), F32),
            V((2, 4, 480, T), F32), V((4, 480, T), F32), V((2, 480, T), F32), V((2, 240, T), F32),
            S((5, NCH)), S((7,)), S((COPIES,)), S((COPIES,)),
        ],
        compiler_params=pltpu.CompilerParams(collective_id=0, has_side_effects=True, vmem_limit_bytes=63 << 20),
        cost_estimate=pl.CostEstimate(flops=24_000_000_000, bytes_accessed=40_000_000, transcendentals=700_000),
    )(
        hidden_in, query_proj, key_proj, value_proj, grad_out,
        query_gain.reshape(1, H), key_gain.reshape(1, H), segment_ids.reshape(1, -1), jnp.asarray(frequency),
    )
    attended, grad_in, grad_query, grad_key, grad_value = pl.pallas_call(
        hand_over, out_shape=outs, in_specs=[hbm] * 5, out_specs=(hbm,) * 5,
        scratch_shapes=[V(out.shape, F32) for out in outs] + [S((2, 5))],
    )(*results)
    return attended, grad_in.T, grad_query, grad_key, grad_value


def solution(mesh):
    return jax.shard_map(
        local,
        mesh=mesh,
        in_specs=(
            P("seq", None), P(None, "tensor"), P(None, "tensor"), P(None, "tensor"), P(), P(), P(), P("seq", "tensor"),
        ),
        out_specs=(P("seq", "tensor"),) * 5,
        check_vma=False,
    )
```

```python
import functools

import jax
import jax.numpy as jnp
import numpy as np
from jax import lax
from jax.experimental import pallas as pl
from jax.experimental.pallas import tpu as pltpu
from jax.sharding import PartitionSpec as P

MESH = pl.DeviceIdType.MESH
WINDOW = 1024
EPS = 1e-06
T = 256
H = 256
D = 3840
NCH = 5
CH = D // NCH
F32, BF16 = jnp.float32, jnp.bfloat16

NN = (((1,), (0,)), ((), ()))
NT = (((1,), (1,)), ((), ()))
TN = (((0,), (0,)), ((), ()))


def split(value):
    high = value.astype(BF16)
    return high, (value - high.astype(F32)).astype(BF16)


def product(left, right, dims):
    (lh, ll), (rh, rl) = left, right
    dot = functools.partial(lax.dot_general, dimension_numbers=dims, preferred_element_type=F32)
    return dot(lh, rh) + (dot(lh, rl) + dot(ll, rh))


def rotate(u, cos, sin):
    a, b = u[:, :128], u[:, 128:]
    return jnp.concatenate([a * cos - b * sin, b * cos + a * sin], axis=1)


def unrotate(u, cos, sin):
    a, b = u[:, :128], u[:, 128:]
    return jnp.concatenate([a * cos + b * sin, b * cos - a * sin], axis=1)


def inv_rms(x):
    return lax.rsqrt(jnp.mean(x * x, axis=1, keepdims=True) + EPS)


def norm_back(x, gain, d_norm):
    r = inv_rms(x)
    gd = d_norm * gain
    return r * gd - x * (r * r * r) * jnp.mean(x * gd, axis=1, keepdims=True)


class Links:
    def __init__(self, send_sems, recv_sems):
        self.sems = send_sems, recv_sems
        self.copies = {}

    def add(self, name, src, dst, device):
        i = len(self.copies)
        self.copies[name] = pltpu.make_async_remote_copy(
            src_ref=src, dst_ref=dst, send_sem=self.sems[0].at[i], recv_sem=self.sems[1].at[i],
            device_id=device, device_id_type=MESH,
        )

    def start(self, *name):
        self.copies[name].start()

    def arrived(self, *name):
        self.copies[name].wait_recv()

    def finish(self):
        for copy in self.copies.values():
            copy.wait_send()


COPIES = 72


def kernel(
    hid_h, wq_h, wk_h, wv_h, grad_h, q_gain_r, k_gain_r, seg, freq_r,
    att_o, gin_o, gq_o, gk_o, gv_o,
    hid, wq, wk, wv, grad, raw, q2, kv, wt, dpt, dqt, contrib, rkv, prev, zr,
    hz, ht_h, ht_l, dc, part, fwd, rpart, term, r1, r2, xfwd, lsem, osem, send_sems, recv_sems,
):
    s = lax.axis_index("seq")
    t = lax.axis_index("tensor")
    z, y = s // 4, lax.rem(s, 4)
    x, c = t // 2, lax.rem(t, 2)

    def at_z(d):
        return (lax.rem(z + d + 4, 4) * 4 + y, t)

    def at_y(d):
        return (z * 4 + lax.rem(y + d + 4, 4), t)

    def at_x(d):
        return (s, lax.rem(x + d + 4, 4) * 2 + c)

    mate = (s, x * 2 + 1 - c)
    barrier = pltpu.get_barrier_semaphore()
    partners = [at_z(1), at_z(2), at_z(3), at_y(1), at_y(2), at_y(3), at_x(1), at_x(2), at_x(3), mate]
    for dev in partners:
        pl.semaphore_signal(barrier, inc=1, device_id=dev, device_id_type=MESH)

    links = Links(send_sems, recv_sems)
    half = pl.ds(pl.multiple_of(c * 128, 128), 128)

    def first_col(zz):
        return ((15 * zz) // 2) * 128

    pieces_of = {0: (pl.ds(0, 128), pl.ds(128, 128)), 1: (pl.ds(0, T),)}
    for kind in (0, 1):
        for i, rows in enumerate(pieces_of[kind]):
            links.add(("kv", 4, kind, i), kv.at[0, kind, rows], kv.at[4, kind, rows], at_z(1))
            for d in (1, 2, 3):
                src = kv.at[4 * ((y + d) // 4), kind, rows]
                links.add(("kv", d, kind, i), src, kv.at[d, kind, rows], at_y(d))
        links.add(("prev", kind), prev.at[kind], zr.at[kind], at_z(-1))
        for d in (1, 2, 3):
            links.add(("back", d, kind), contrib.at[d, kind], rkv.at[d - 1, kind], at_y(-d))
    for d in (1, 2, 3):
        cols = pl.ds(pl.multiple_of(first_col(lax.rem(z + d, 4)), 128), 1024)
        links.add(("hid", d), hid.at[half, cols], hz.at[d - 1, half], at_z(d))
        links.add(("hid_mate", d), hz.at[d - 1, half], hz.at[d - 1, half], mate)
    for k in range(4):
        links.add(("core", k), term.at[1, k], r1.at[k], mate)
    for i, d in enumerate((1, 3)):
        rows = pl.ds(240 * i, 240)
        links.add(("x_fwd", d), term.at[0, 2, rows], xfwd.at[i], at_x(d))
        links.add(("x", d), term.at[0, d], r2.at[i], at_x(d))
    spans = {"q0": pl.ds(0, H), "q1": pl.ds(H, H), "k": pl.ds(2 * H, H), "v": pl.ds(3 * H, H)}
    for g, cols in spans.items():
        links.add(("dc", g, 1), dc.at[0, :, cols], dc.at[1, :, cols], at_z(1))
        links.add(("dc", g, 3), dc.at[0, :, cols], dc.at[3, :, cols], at_z(-1))
        links.add(("dc2", g, 1), dc.at[1, :128, cols], dc.at[2, :128, cols], at_z(1))
        links.add(("dc2", g, 3), dc.at[3, 128:, cols], dc.at[2, 128:, cols], at_z(-1))
    for g in range(4):
        links.add(("fwd", g, 1), part.at[2, g, :120], fwd.at[0, g], at_y(1))
        links.add(("fwd", g, 3), part.at[2, g, 120:], fwd.at[1, g], at_y(-1))
        links.add(("sum", g, 1), part.at[1, g], rpart.at[0, g], at_y(1))
        links.add(("sum", g, 3), part.at[3, g], rpart.at[1, g], at_y(-1))

    writes = []

    def write(i, src, dst):
        copy = pltpu.make_async_copy(src, dst, osem.at[i])
        copy.start()
        writes.append(copy)

    def columns(i):
        return pl.ds(pl.multiple_of(i * CH, CH), CH)

    def local_copy(j, i):
        if j == 0:
            return pltpu.make_async_copy(hid_h.at[:, columns(i)], hid.at[:, columns(i)], lsem.at[0, i])
        src, dst = ((wk_h, wk), (wv_h, wv), (wq_h, wq))[j - 1]
        return pltpu.make_async_copy(src.at[columns(i)], dst.at[columns(i)], lsem.at[j, i])

    for i in range(NCH):
        local_copy(0, i).start()
        local_copy(1, i).start()
    for j in (2, 3):
        for i in range(NCH):
            local_copy(j, i).start()
    grad_copy = pltpu.make_async_copy(grad_h, grad, lsem.at[4, 0])
    grad_copy.start()

    place = (s * T + lax.broadcasted_iota(jnp.int32, (T, H // 2), 0)).astype(F32)
    angle = place * freq_r[...]
    cos, sin = jnp.cos(angle), jnp.sin(angle)
    q_gain, k_gain = q_gain_r[...], k_gain_r[...]

    def project(j, weight, col, load_hid, load_w):
        def step(i, acc):
            if load_hid:
                local_copy(0, i).wait()
            if load_w:
                local_copy(j, i).wait()
            left = split(hid[:, columns(i)])
            right = split(weight[columns(i), col : col + H])
            return acc + product(left, right, NN)

        return lax.fori_loop(0, NCH, step, jnp.zeros((T, H), F32))

    def send_own(kind):
        for i in range(len(pieces_of[kind])):
            links.start("kv", 4, kind, i)
        for d in (1, 2, 3):
            @pl.when(y + d < 4)
            def _():
                for i in range(len(pieces_of[kind])):
                    links.start("kv", d, kind, i)

    def send_prev(kind):
        for i in range(len(pieces_of[kind])):
            links.arrived("kv", 4, kind, i)
            for d in (1, 2, 3):
                @pl.when(y + d >= 4)
                def _():
                    links.start("kv", d, kind, i)

    def have(d, kind):
        if d in (1, 2, 3):
            for i in range(len(pieces_of[kind])):
                links.arrived("kv", d, kind, i)

    key_raw = project(1, wk, 0, True, True)
    raw[2] = key_raw
    kv[0, 0] = rotate(key_raw * inv_rms(key_raw) * k_gain, cos, sin)
    pl.semaphore_wait(barrier, len(partners))
    send_own(0)
    kv[0, 1] = project(2, wv, 0, False, True)
    send_own(1)

    def query(h, load):
        q_raw = project(3, wq, h * H, False, load)
        raw[h] = q_raw
        q2[h * T : (h + 1) * T, :] = rotate(q_raw * inv_rms(q_raw) * q_gain, cos, sin) * (H ** -0.5)

    query(0, True)
    send_prev(0)
    query(1, False)
    send_prev(1)
    grad_copy.wait()

    for d in (1, 2, 3):
        links.start("hid", d)

    def q_pair():
        return split(q2[...])

    def g_pair():
        return split(jnp.concatenate([grad[:, :H], grad[:, H:]], axis=0))

    row = lax.broadcasted_iota(jnp.int32, (T, 2 * T), 0)
    col = lax.rem(lax.broadcasted_iota(jnp.int32, (T, 2 * T), 1), T)

    def segments(blk):
        return seg[:, pl.ds(pl.multiple_of(blk * T, T), T)]

    seg_q = segments(s)
    seg_q = jnp.concatenate([seg_q, seg_q], axis=1)

    def weigh(d):
        seg_k = jnp.broadcast_to(segments(lax.rem(s - d + 16, 16)), (T, T)).T
        seg_k = jnp.concatenate([seg_k, seg_k], axis=1)
        dist = 256 * d + col - row
        allowed = (dist >= 0) & (dist < WINDOW) & (seg_k == seg_q) & (s - d >= 0)
        scores = product(split(kv[d, 0]), q_pair(), NT)
        weights = jnp.where(allowed, jnp.exp(scores), 0.0)
        wt[d] = weights
        return jnp.sum(weights, axis=0, keepdims=True)

    def weigh_values(d):
        d_shares = product(split(kv[d, 1]), g_pair(), NT)
        dpt[d] = d_shares
        return jnp.sum(wt[d] * d_shares, axis=0, keepdims=True)

    total = delta = jnp.zeros((1, 2 * T), F32)
    for d in (0, 4):
        total = total + weigh(d)
    for d in (0, 4):
        delta = delta + weigh_values(d)
    for d in (1, 3, 2):
        have(d, 0)
        total = total + weigh(d)
        have(d, 1)
        delta = delta + weigh_values(d)
    inverse = 1.0 / total
    delta = delta * inverse

    def back_values(d):
        shares = wt[d] * inverse
        wt[d] = shares
        contrib[d, 1] = product(split(shares), g_pair(), NN)

    def back_keys(d, first):
        d_scores = split(wt[d] * (dpt[d] - delta))
        contrib[d, 0] = product(d_scores, q_pair(), NN)
        if d in (1, 2, 3):
            links.start("back", d, 0)
        more = product(split(kv[d, 0]), d_scores, TN)
        dqt[...] = more if first else dqt[...] + more

    for d in (2, 1, 3):
        back_values(d)
        links.start("back", d, 1)
    for d in (2, 1, 3):
        back_keys(d, d == 2)
    for d in (4, 0):
        back_values(d)
        back_keys(d, False)
    d_q = dqt[...].T * (H ** -0.5)
    def spread(g):
        links.start("dc", g, 1)
        links.start("dc", g, 3)

    def spread_on(g):
        for d in (1, 3):
            links.arrived("dc", g, d)
            links.start("dc2", g, d)

    def gathered(g):
        for d in (1, 3):
            links.arrived("dc2", g, d)

    for h, g in ((0, "q0"), (1, "q1")):
        dc[0, :, h * H : (h + 1) * H] = norm_back(raw[h], q_gain, unrotate(d_q[h * T : (h + 1) * T], cos, sin))
        spread(g)

    out_t = None
    for d in range(5):
        more = product(split(kv[d, 1]), split(wt[d]), TN)
        out_t = more if out_t is None else out_t + more
    q2[...] = out_t.T
    for h in (0, 1):
        write(h, q2.at[h * T : (h + 1) * T], att_o.at[:, h * H : (h + 1) * H])

    for d in (1, 2, 3):
        links.arrived("hid", d)
        links.start("hid_mate", d)

    def transpose_into(d, read):
        def step(i, carry):
            lanes = pl.multiple_of(i * 256, 256)
            high, low = split(read(lanes).T)
            ht_h[pl.ds(lanes, 256), d * T : (d + 1) * T] = high
            ht_l[pl.ds(lanes, 256), d * T : (d + 1) * T] = low
            return carry

        lax.fori_loop(0, 4, step, 0)

    base = first_col(z)
    transpose_into(0, lambda lanes: hid[:, pl.ds(pl.multiple_of(base + lanes, 128), 256)])
    for d in (1, 2, 3):
        links.arrived("hid_mate", d)
        transpose_into(d, lambda lanes: hz[d - 1, :, pl.ds(lanes, 256)])

    weights = [(wq, 0), (wq, H), (wk, 0), (wv, 0)]

    def input_part(k, core, grads):
        rows = pl.ds(pl.multiple_of((2 * lax.rem(x + k, 4) + core) * 480, 32), 480)
        acc = None
        for g, grad_g in grads.items():
            w, first = weights[g]
            one = product(split(w[rows, first : first + H]), grad_g, NT)
            acc = one if acc is None else acc + one
        return acc

    q_own = {g: split(dc[0, :, g * H : (g + 1) * H]) for g in (0, 1)}
    spread_on("q0")
    for k in range(4):
        term[0, k] = input_part(k, c, q_own)
        if k == 1:
            spread_on("q1")
        term[1, k] = input_part(k, 1 - c, q_own)

    def collect(kind):
        mine, before = contrib[0, kind], contrib[4, kind]
        for d in (1, 2, 3):
            links.arrived("back", d, kind)
            got = rkv[d - 1, kind]
            inside = jnp.where(y + d < 4, 1.0, 0.0).astype(F32)
            mine = mine + inside * got
            before = before + (1.0 - inside) * got
        prev[kind] = before
        contrib[0, kind] = mine
        links.start("prev", kind)

    collect(1)

    off = lax.rem(z, 2) * 64

    def send_far(g):
        links.start("fwd", g, 1)
        links.start("fwd", g, 3)

    def partial(g):
        pieces = [split(dc[k, :, g * H : (g + 1) * H]) for k in range(4)]
        right = tuple(jnp.concatenate([p[i] for p in pieces], axis=0) for i in (0, 1))
        for d in (2, 1, 3, 0):
            rows = pl.ds(pl.multiple_of(off + 240 * lax.rem(y + d, 4), 16), 240)
            part[d, g] = product((ht_h[rows, :], ht_l[rows, :]), right, NN)
            if d == 2 and g > 1:
                send_far(g)

    def pass_on(g):
        links.arrived("fwd", g, 1)
        part[1, g, :120] = part[1, g, :120] + fwd[0, g]
        links.start("sum", g, 1)
        links.arrived("fwd", g, 3)
        part[3, g, 120:] = part[3, g, 120:] + fwd[1, g]
        links.start("sum", g, 3)

    def summed(g):
        links.arrived("sum", g, 1)
        links.arrived("sum", g, 3)
        part[0, g] = part[0, g] + (rpart[0, g] + rpart[1, g])
        dst = (gq_o.at[:, :H], gq_o.at[:, H:], gk_o, gv_o)[g]
        write(2 + g, part.at[0, g], dst)

    gathered("q0")
    partial(0)
    gathered("q1")
    partial(1)
    collect(0)
    send_far(0)
    send_far(1)

    links.arrived("prev", 1)
    dc[0, :, 3 * H : 4 * H] = contrib[0, 1] + zr[1]
    spread("v")
    links.arrived("prev", 0)
    d_key = unrotate(contrib[0, 0] + zr[0], cos, sin)
    dc[0, :, 2 * H : 3 * H] = norm_back(raw[2], k_gain, d_key)
    spread("k")
    pass_on(0)
    pass_on(1)

    kv_own = {g: split(dc[0, :, g * H : (g + 1) * H]) for g in (2, 3)}

    def other(k):
        term[1, k] = term[1, k] + input_part(k, 1 - c, kv_own)
        links.start("core", k)

    def both(k):
        mine = term[0, k] + input_part(k, c, kv_own)
        links.arrived("core", k)
        term[0, k] = mine + r1[k]

    other(2)
    other(1)
    both(2)
    for d in (1, 3):
        links.start("x_fwd", d)
    spread_on("v")
    other(3)
    other(0)
    for k in (1, 3, 0):
        both(k)

    gathered("v")
    partial(3)
    spread_on("k")
    for i, d in enumerate((1, 3)):
        links.arrived("x_fwd", d)
        rows = pl.ds(240 * i, 240)
        term[0, d, rows] = term[0, d, rows] + xfwd[i]
        links.start("x", d)
    gathered("k")
    partial(2)
    pass_on(3)
    pass_on(2)

    summed(0)
    summed(1)
    links.arrived("x", 1)
    links.arrived("x", 3)
    term[0, 0] = term[0, 0] + (r2[0] + r2[1])
    write(6, term.at[0, 0], gin_o)
    summed(3)
    summed(2)
    for copy in writes:
        copy.wait()
    links.finish()


def hand_over(*refs):
    ins, outs, held, sems = refs[:5], refs[5:10], refs[10:15], refs[15]
    loads = [pltpu.make_async_copy(ins[i], held[i], sems.at[0, i]) for i in range(5)]
    stores = [pltpu.make_async_copy(held[i], outs[i], sems.at[1, i]) for i in range(5)]
    for load in loads:
        load.start()
    for load, store in zip(loads, stores):
        load.wait()
        store.start()
    for store in stores:
        store.wait()


def local(hidden_in, query_proj, key_proj, value_proj, query_gain, key_gain, segment_ids, grad_out):
    frequency = np.power(10000.0, -2.0 * np.arange(H // 2) / H).astype(np.float32)[None, :]
    vmem = pl.BlockSpec(memory_space=pltpu.VMEM)
    hbm = pl.BlockSpec(memory_space=pl.ANY)
    V, S = pltpu.VMEM, pltpu.SemaphoreType.DMA
    shape = jax.ShapeDtypeStruct
    outs = (
        shape((T, 512), F32), shape((480, T), F32), shape((240, 512), F32), shape((240, 256), F32), shape((240, 256), F32),
    )
    results = pl.pallas_call(
        kernel,
        out_shape=outs,
        in_specs=[hbm] * 5 + [vmem] * 4,
        out_specs=(hbm,) * 5,
        scratch_shapes=[
            V((T, D), F32), V((D, 512), F32), V((D, 256), F32), V((D, 256), F32), V((T, 512), F32),
            V((3, T, H), F32), V((2 * T, H), F32), V((5, 2, T, H), F32), V((5, T, 2 * T), F32), V((5, T, 2 * T), F32),
            V((H, 2 * T), F32), V((5, 2, T, H), F32), V((3, 2, T, H), F32), V((2, T, H), F32), V((2, T, H), F32),
            V((3, T, 1024), F32), V((1024, 1024), BF16), V((1024, 1024), BF16), V((4, T, 1024), F32),
            V((4, 4, 240, H), F32), V((2, 4, 120, H), F32), V((2, 4, 240, H), F32),
            V((2, 4, 480, T), F32), V((4, 480, T), F32), V((2, 480, T), F32), V((2, 240, T), F32),
            S((5, NCH)), S((7,)), S((COPIES,)), S((COPIES,)),
        ],
        compiler_params=pltpu.CompilerParams(collective_id=0, has_side_effects=True, vmem_limit_bytes=63 << 20),
        cost_estimate=pl.CostEstimate(flops=24_000_000_000, bytes_accessed=40_000_000, transcendentals=700_000),
    )(
        hidden_in, query_proj, key_proj, value_proj, grad_out,
        query_gain.reshape(1, H), key_gain.reshape(1, H), segment_ids.reshape(1, -1), jnp.asarray(frequency),
    )
    attended, grad_in, grad_query, grad_key, grad_value = pl.pallas_call(
        hand_over, out_shape=outs, in_specs=[hbm] * 5, out_specs=(hbm,) * 5,
        scratch_shapes=[V(out.shape, F32) for out in outs] + [S((2, 5))],
    )(*results)
    return attended, grad_in.T, grad_query, grad_key, grad_value


def solution(mesh):
    return jax.shard_map(
        local,
        mesh=mesh,
        in_specs=(
            P("seq", None), P(None, "tensor"), P(None, "tensor"), P(None, "tensor"), P(), P(), P(), P("seq", "tensor"),
        ),
        out_specs=(P("seq", "tensor"),) * 5,
        check_vma=False,
    )
```

```python
import functools

import jax
import jax.numpy as jnp
import numpy as np
from jax import lax
from jax.experimental import pallas as pl
from jax.experimental.pallas import tpu as pltpu
from jax.sharding import PartitionSpec as P

MESH = pl.DeviceIdType.MESH
WINDOW = 1024
EPS = 1e-06
T = 256
H = 256
D = 3840
NCH = 5
CH = D // NCH
F32, BF16 = jnp.float32, jnp.bfloat16

NN = (((1,), (0,)), ((), ()))
NT = (((1,), (1,)), ((), ()))
TN = (((0,), (0,)), ((), ()))


def split(value):
    high = value.astype(BF16)
    return high, (value - high.astype(F32)).astype(BF16)


def product(left, right, dims):
    (lh, ll), (rh, rl) = left, right
    dot = functools.partial(lax.dot_general, dimension_numbers=dims, preferred_element_type=F32)
    return dot(lh, rh) + (dot(lh, rl) + dot(ll, rh))


def rotate(u, cos, sin):
    a, b = u[:, :128], u[:, 128:]
    return jnp.concatenate([a * cos - b * sin, b * cos + a * sin], axis=1)


def unrotate(u, cos, sin):
    a, b = u[:, :128], u[:, 128:]
    return jnp.concatenate([a * cos + b * sin, b * cos - a * sin], axis=1)


def inv_rms(x):
    return lax.rsqrt(jnp.mean(x * x, axis=1, keepdims=True) + EPS)


def norm_back(x, gain, d_norm):
    r = inv_rms(x)
    gd = d_norm * gain
    return r * gd - x * (r * r * r) * jnp.mean(x * gd, axis=1, keepdims=True)


class Links:
    def __init__(self, send_sems, recv_sems):
        self.sems = send_sems, recv_sems
        self.copies = {}

    def add(self, name, src, dst, device):
        i = len(self.copies)
        self.copies[name] = pltpu.make_async_remote_copy(
            src_ref=src, dst_ref=dst, send_sem=self.sems[0].at[i], recv_sem=self.sems[1].at[i],
            device_id=device, device_id_type=MESH,
        )

    def start(self, *name):
        self.copies[name].start()

    def arrived(self, *name):
        self.copies[name].wait_recv()

    def finish(self):
        for copy in self.copies.values():
            copy.wait_send()


COPIES = 72


def kernel(
    hid_h, wq_h, wk_h, wv_h, grad_h, q_gain_r, k_gain_r, seg, freq_r,
    att_o, gin_o, gq_o, gk_o, gv_o,
    hid, wq, wk, wv, grad, raw, q2, kv, wt, dpt, dqt, contrib, rkv, prev, zr,
    hz, ht_h, ht_l, dc, part, fwd, rpart, term, r1, r2, xfwd, lsem, osem, send_sems, recv_sems,
):
    s = lax.axis_index("seq")
    t = lax.axis_index("tensor")
    z, y = s // 4, lax.rem(s, 4)
    x, c = t // 2, lax.rem(t, 2)

    def at_z(d):
        return (lax.rem(z + d + 4, 4) * 4 + y, t)

    def at_y(d):
        return (z * 4 + lax.rem(y + d + 4, 4), t)

    def at_x(d):
        return (s, lax.rem(x + d + 4, 4) * 2 + c)

    mate = (s, x * 2 + 1 - c)
    barrier = pltpu.get_barrier_semaphore()
    partners = [at_z(1), at_z(2), at_z(3), at_y(1), at_y(2), at_y(3), at_x(1), at_x(2), at_x(3), mate]
    for dev in partners:
        pl.semaphore_signal(barrier, inc=1, device_id=dev, device_id_type=MESH)

    links = Links(send_sems, recv_sems)
    half = pl.ds(pl.multiple_of(c * 128, 128), 128)

    def first_col(zz):
        return ((15 * zz) // 2) * 128

    pieces_of = {0: (pl.ds(0, 128), pl.ds(128, 128)), 1: (pl.ds(0, T),)}
    for kind in (0, 1):
        for i, rows in enumerate(pieces_of[kind]):
            links.add(("kv", 4, kind, i), kv.at[0, kind, rows], kv.at[4, kind, rows], at_z(1))
            for d in (1, 2, 3):
                src = kv.at[4 * ((y + d) // 4), kind, rows]
                links.add(("kv", d, kind, i), src, kv.at[d, kind, rows], at_y(d))
        links.add(("prev", kind), prev.at[kind], zr.at[kind], at_z(-1))
        for d in (1, 2, 3):
            links.add(("back", d, kind), contrib.at[d, kind], rkv.at[d - 1, kind], at_y(-d))
    for d in (1, 2, 3):
        cols = pl.ds(pl.multiple_of(first_col(lax.rem(z + d, 4)), 128), 1024)
        links.add(("hid", d), hid.at[half, cols], hz.at[d - 1, half], at_z(d))
        links.add(("hid_mate", d), hz.at[d - 1, half], hz.at[d - 1, half], mate)
    for k in range(4):
        links.add(("core", k), term.at[1, k], r1.at[k], mate)
    for i, d in enumerate((1, 3)):
        rows = pl.ds(240 * i, 240)
        links.add(("x_fwd", d), term.at[0, 2, rows], xfwd.at[i], at_x(d))
        links.add(("x", d), term.at[0, d], r2.at[i], at_x(d))
    spans = {"q0": pl.ds(0, H), "q1": pl.ds(H, H), "k": pl.ds(2 * H, H), "v": pl.ds(3 * H, H)}
    for g, cols in spans.items():
        links.add(("dc", g, 1), dc.at[0, :, cols], dc.at[1, :, cols], at_z(1))
        links.add(("dc", g, 3), dc.at[0, :, cols], dc.at[3, :, cols], at_z(-1))
        cut = 128 if g in ("q0", "q1") else 192
        links.add(("dc2", g, 1), dc.at[1, :cut, cols], dc.at[2, :cut, cols], at_z(1))
        links.add(("dc2", g, 3), dc.at[3, cut:, cols], dc.at[2, cut:, cols], at_z(-1))
    for g in range(4):
        links.add(("fwd", g, 1), part.at[2, g, :120], fwd.at[0, g], at_y(1))
        links.add(("fwd", g, 3), part.at[2, g, 120:], fwd.at[1, g], at_y(-1))
        links.add(("sum", g, 1), part.at[1, g], rpart.at[0, g], at_y(1))
        links.add(("sum", g, 3), part.at[3, g], rpart.at[1, g], at_y(-1))

    writes = []

    def write(i, src, dst):
        copy = pltpu.make_async_copy(src, dst, osem.at[i])
        copy.start()
        writes.append(copy)

    def columns(i):
        return pl.ds(pl.multiple_of(i * CH, CH), CH)

    def local_copy(j, i):
        if j == 0:
            return pltpu.make_async_copy(hid_h.at[:, columns(i)], hid.at[:, columns(i)], lsem.at[0, i])
        src, dst = ((wk_h, wk), (wv_h, wv), (wq_h, wq))[j - 1]
        return pltpu.make_async_copy(src.at[columns(i)], dst.at[columns(i)], lsem.at[j, i])

    for i in range(NCH):
        local_copy(0, i).start()
        local_copy(1, i).start()
    for j in (2, 3):
        for i in range(NCH):
            local_copy(j, i).start()
    grad_copy = pltpu.make_async_copy(grad_h, grad, lsem.at[4, 0])
    grad_copy.start()

    place = (s * T + lax.broadcasted_iota(jnp.int32, (T, H // 2), 0)).astype(F32)
    angle = place * freq_r[...]
    cos, sin = jnp.cos(angle), jnp.sin(angle)
    q_gain, k_gain = q_gain_r[...], k_gain_r[...]

    def project(j, weight, col, load_hid, load_w):
        def step(i, acc):
            if load_hid:
                local_copy(0, i).wait()
            if load_w:
                local_copy(j, i).wait()
            left = split(hid[:, columns(i)])
            right = split(weight[columns(i), col : col + H])
            return acc + product(left, right, NN)

        return lax.fori_loop(0, NCH, step, jnp.zeros((T, H), F32))

    def send_own(kind):
        for i in range(len(pieces_of[kind])):
            links.start("kv", 4, kind, i)
        for d in (1, 2, 3):
            @pl.when(y + d < 4)
            def _():
                for i in range(len(pieces_of[kind])):
                    links.start("kv", d, kind, i)

    def send_prev(kind):
        for i in range(len(pieces_of[kind])):
            links.arrived("kv", 4, kind, i)
            for d in (1, 2, 3):
                @pl.when(y + d >= 4)
                def _():
                    links.start("kv", d, kind, i)

    def have(d, kind):
        if d in (1, 2, 3):
            for i in range(len(pieces_of[kind])):
                links.arrived("kv", d, kind, i)

    key_raw = project(1, wk, 0, True, True)
    raw[2] = key_raw
    kv[0, 0] = rotate(key_raw * inv_rms(key_raw) * k_gain, cos, sin)
    pl.semaphore_wait(barrier, len(partners))
    send_own(0)
    kv[0, 1] = project(2, wv, 0, False, True)
    send_own(1)

    def query(h, load):
        q_raw = project(3, wq, h * H, False, load)
        raw[h] = q_raw
        q2[h * T : (h + 1) * T, :] = rotate(q_raw * inv_rms(q_raw) * q_gain, cos, sin) * (H ** -0.5)

    query(0, True)
    send_prev(0)
    query(1, False)
    send_prev(1)
    grad_copy.wait()

    for d in (1, 2, 3):
        links.start("hid", d)

    def q_pair():
        return split(q2[...])

    def g_pair():
        return split(jnp.concatenate([grad[:, :H], grad[:, H:]], axis=0))

    row = lax.broadcasted_iota(jnp.int32, (T, 2 * T), 0)
    col = lax.rem(lax.broadcasted_iota(jnp.int32, (T, 2 * T), 1), T)

    def segments(blk):
        return seg[:, pl.ds(pl.multiple_of(blk * T, T), T)]

    seg_q = segments(s)
    seg_q = jnp.concatenate([seg_q, seg_q], axis=1)

    def weigh(d):
        seg_k = jnp.broadcast_to(segments(lax.rem(s - d + 16, 16)), (T, T)).T
        seg_k = jnp.concatenate([seg_k, seg_k], axis=1)
        dist = 256 * d + col - row
        allowed = (dist >= 0) & (dist < WINDOW) & (seg_k == seg_q) & (s - d >= 0)
        scores = product(split(kv[d, 0]), q_pair(), NT)
        weights = jnp.where(allowed, jnp.exp(scores), 0.0)
        wt[d] = weights
        return jnp.sum(weights, axis=0, keepdims=True)

    def weigh_values(d):
        d_shares = product(split(kv[d, 1]), g_pair(), NT)
        dpt[d] = d_shares
        return jnp.sum(wt[d] * d_shares, axis=0, keepdims=True)

    total = delta = jnp.zeros((1, 2 * T), F32)
    for d in (0, 4):
        total = total + weigh(d)
    for d in (0, 4):
        delta = delta + weigh_values(d)
    for d in (1, 3, 2):
        have(d, 0)
        total = total + weigh(d)
        have(d, 1)
        delta = delta + weigh_values(d)
    inverse = 1.0 / total
    delta = delta * inverse

    def back_values(d):
        shares = wt[d] * inverse
        wt[d] = shares
        contrib[d, 1] = product(split(shares), g_pair(), NN)

    def back_scores(d):
        d_scores = wt[d] * (dpt[d] - delta)
        dpt[d] = d_scores
        return product(split(kv[d, 0]), split(d_scores), TN)

    def back_keys(d):
        contrib[d, 0] = product(split(dpt[d]), q_pair(), NN)
        if d in (1, 2, 3):
            links.start("back", d, 0)

    for d in (2, 1, 3):
        back_values(d)
        links.start("back", d, 1)
    for d in (4, 0):
        wt[d] = wt[d] * inverse
    dqt[...] = back_scores(0)
    for d in (1, 2, 3, 4):
        dqt[...] = dqt[...] + back_scores(d)

    def spread(g):
        links.start("dc", g, 1)
        links.start("dc", g, 3)

    def spread_on(g):
        for d in (1, 3):
            links.arrived("dc", g, d)
            links.start("dc2", g, d)

    def gathered(g):
        for d in (1, 3):
            links.arrived("dc2", g, d)

    for h, g in ((0, "q0"), (1, "q1")):
        d_q = dqt[:, h * T : (h + 1) * T].T * (H ** -0.5)
        dc[0, :, h * H : (h + 1) * H] = norm_back(raw[h], q_gain, unrotate(d_q, cos, sin))
        spread(g)
    for d in (2, 1, 3):
        back_keys(d)
    for d in (4, 0):
        contrib[d, 1] = product(split(wt[d]), g_pair(), NN)
        back_keys(d)

    out_t = None
    for d in range(5):
        more = product(split(kv[d, 1]), split(wt[d]), TN)
        out_t = more if out_t is None else out_t + more
    q2[...] = out_t.T
    for h in (0, 1):
        write(h, q2.at[h * T : (h + 1) * T], att_o.at[:, h * H : (h + 1) * H])

    for d in (1, 2, 3):
        links.arrived("hid", d)
        links.start("hid_mate", d)

    def transpose_into(d, read):
        def step(i, carry):
            lanes = pl.multiple_of(i * 256, 256)
            high, low = split(read(lanes).T)
            ht_h[pl.ds(lanes, 256), d * T : (d + 1) * T] = high
            ht_l[pl.ds(lanes, 256), d * T : (d + 1) * T] = low
            return carry

        lax.fori_loop(0, 4, step, 0)

    base = first_col(z)
    transpose_into(0, lambda lanes: hid[:, pl.ds(pl.multiple_of(base + lanes, 128), 256)])
    for d in (1, 2, 3):
        links.arrived("hid_mate", d)
        transpose_into(d, lambda lanes: hz[d - 1, :, pl.ds(lanes, 256)])

    weights = [(wq, 0), (wq, H), (wk, 0), (wv, 0)]

    def input_part(k, core, grads):
        rows = pl.ds(pl.multiple_of((2 * lax.rem(x + k, 4) + core) * 480, 32), 480)
        acc = None
        for g, grad_g in grads.items():
            w, first = weights[g]
            one = product(split(w[rows, first : first + H]), grad_g, NT)
            acc = one if acc is None else acc + one
        return acc

    q_own = {g: split(dc[0, :, g * H : (g + 1) * H]) for g in (0, 1)}
    spread_on("q0")
    for k in range(4):
        term[0, k] = input_part(k, c, q_own)
        if k == 1:
            spread_on("q1")
        term[1, k] = input_part(k, 1 - c, q_own)

    def collect(kind):
        mine, before = contrib[0, kind], contrib[4, kind]
        for d in (1, 2, 3):
            links.arrived("back", d, kind)
            got = rkv[d - 1, kind]
            inside = jnp.where(y + d < 4, 1.0, 0.0).astype(F32)
            mine = mine + inside * got
            before = before + (1.0 - inside) * got
        prev[kind] = before
        contrib[0, kind] = mine
        links.start("prev", kind)

    collect(1)

    off = lax.rem(z, 2) * 64

    def send_far(g):
        links.start("fwd", g, 1)
        links.start("fwd", g, 3)

    def partial(g):
        pieces = [split(dc[k, :, g * H : (g + 1) * H]) for k in range(4)]
        right = tuple(jnp.concatenate([p[i] for p in pieces], axis=0) for i in (0, 1))
        for d in (2, 1, 3, 0):
            rows = pl.ds(pl.multiple_of(off + 240 * lax.rem(y + d, 4), 16), 240)
            part[d, g] = product((ht_h[rows, :], ht_l[rows, :]), right, NN)
            if d == 2 and g > 1:
                send_far(g)

    def pass_on(g):
        links.arrived("fwd", g, 1)
        part[1, g, :120] = part[1, g, :120] + fwd[0, g]
        links.start("sum", g, 1)
        links.arrived("fwd", g, 3)
        part[3, g, 120:] = part[3, g, 120:] + fwd[1, g]
        links.start("sum", g, 3)

    def summed(g):
        links.arrived("sum", g, 1)
        links.arrived("sum", g, 3)
        part[0, g] = part[0, g] + (rpart[0, g] + rpart[1, g])
        dst = (gq_o.at[:, :H], gq_o.at[:, H:], gk_o, gv_o)[g]
        write(2 + g, part.at[0, g], dst)

    gathered("q0")
    partial(0)
    gathered("q1")
    partial(1)
    collect(0)
    send_far(0)
    send_far(1)

    links.arrived("prev", 1)
    dc[0, :, 3 * H : 4 * H] = contrib[0, 1] + zr[1]
    spread("v")
    links.arrived("prev", 0)
    d_key = unrotate(contrib[0, 0] + zr[0], cos, sin)
    dc[0, :, 2 * H : 3 * H] = norm_back(raw[2], k_gain, d_key)
    spread("k")
    pass_on(0)
    pass_on(1)

    kv_own = {g: split(dc[0, :, g * H : (g + 1) * H]) for g in (2, 3)}

    def other(k):
        term[1, k] = term[1, k] + input_part(k, 1 - c, kv_own)
        links.start("core", k)

    def both(k):
        mine = term[0, k] + input_part(k, c, kv_own)
        links.arrived("core", k)
        term[0, k] = mine + r1[k]

    other(2)
    other(1)
    both(2)
    for d in (1, 3):
        links.start("x_fwd", d)
    spread_on("v")
    other(3)
    other(0)
    for k in (1, 3, 0):
        both(k)

    gathered("v")
    partial(3)
    spread_on("k")
    for i, d in enumerate((1, 3)):
        links.arrived("x_fwd", d)
        rows = pl.ds(240 * i, 240)
        term[0, d, rows] = term[0, d, rows] + xfwd[i]
        links.start("x", d)
    gathered("k")
    partial(2)
    pass_on(3)
    pass_on(2)

    summed(0)
    summed(1)
    links.arrived("x", 1)
    links.arrived("x", 3)
    term[0, 0] = term[0, 0] + (r2[0] + r2[1])
    write(6, term.at[0, 0], gin_o)
    summed(3)
    summed(2)
    for copy in writes:
        copy.wait()
    links.finish()


def hand_over(*refs):
    ins, outs, held, sems = refs[:5], refs[5:10], refs[10:15], refs[15]
    loads = [pltpu.make_async_copy(ins[i], held[i], sems.at[0, i]) for i in range(5)]
    stores = [pltpu.make_async_copy(held[i], outs[i], sems.at[1, i]) for i in range(5)]
    for load in loads:
        load.start()
    for load, store in zip(loads, stores):
        load.wait()
        store.start()
    for store in stores:
        store.wait()


def local(hidden_in, query_proj, key_proj, value_proj, query_gain, key_gain, segment_ids, grad_out):
    frequency = np.power(10000.0, -2.0 * np.arange(H // 2) / H).astype(np.float32)[None, :]
    vmem = pl.BlockSpec(memory_space=pltpu.VMEM)
    hbm = pl.BlockSpec(memory_space=pl.ANY)
    V, S = pltpu.VMEM, pltpu.SemaphoreType.DMA
    shape = jax.ShapeDtypeStruct
    outs = (
        shape((T, 512), F32), shape((480, T), F32), shape((240, 512), F32), shape((240, 256), F32), shape((240, 256), F32),
    )
    results = pl.pallas_call(
        kernel,
        out_shape=outs,
        in_specs=[hbm] * 5 + [vmem] * 4,
        out_specs=(hbm,) * 5,
        scratch_shapes=[
            V((T, D), F32), V((D, 512), F32), V((D, 256), F32), V((D, 256), F32), V((T, 512), F32),
            V((3, T, H), F32), V((2 * T, H), F32), V((5, 2, T, H), F32), V((5, T, 2 * T), F32), V((5, T, 2 * T), F32),
            V((H, 2 * T), F32), V((5, 2, T, H), F32), V((3, 2, T, H), F32), V((2, T, H), F32), V((2, T, H), F32),
            V((3, T, 1024), F32), V((1024, 1024), BF16), V((1024, 1024), BF16), V((4, T, 1024), F32),
            V((4, 4, 240, H), F32), V((2, 4, 120, H), F32), V((2, 4, 240, H), F32),
            V((2, 4, 480, T), F32), V((4, 480, T), F32), V((2, 480, T), F32), V((2, 240, T), F32),
            S((5, NCH)), S((7,)), S((COPIES,)), S((COPIES,)),
        ],
        compiler_params=pltpu.CompilerParams(collective_id=0, has_side_effects=True, vmem_limit_bytes=63 << 20),
        cost_estimate=pl.CostEstimate(flops=24_000_000_000, bytes_accessed=40_000_000, transcendentals=700_000),
    )(
        hidden_in, query_proj, key_proj, value_proj, grad_out,
        query_gain.reshape(1, H), key_gain.reshape(1, H), segment_ids.reshape(1, -1), jnp.asarray(frequency),
    )
    attended, grad_in, grad_query, grad_key, grad_value = pl.pallas_call(
        hand_over, out_shape=outs, in_specs=[hbm] * 5, out_specs=(hbm,) * 5,
        scratch_shapes=[V(out.shape, F32) for out in outs] + [S((2, 5))],
    )(*results)
    return attended, grad_in.T, grad_query, grad_key, grad_value


def solution(mesh):
    return jax.shard_map(
        local,
        mesh=mesh,
        in_specs=(
            P("seq", None), P(None, "tensor"), P(None, "tensor"), P(None, "tensor"), P(), P(), P(), P("seq", "tensor"),
        ),
        out_specs=(P("seq", "tensor"),) * 5,
        check_vma=False,
    )
```

```python
import functools

import jax
import jax.numpy as jnp
import numpy as np
from jax import lax
from jax.experimental import pallas as pl
from jax.experimental.pallas import tpu as pltpu
from jax.sharding import PartitionSpec as P

MESH = pl.DeviceIdType.MESH
WINDOW = 1024
EPS = 1e-06
T = 256
H = 256
D = 3840
NCH = 5
CH = D // NCH
F32, BF16 = jnp.float32, jnp.bfloat16

NN = (((1,), (0,)), ((), ()))
NT = (((1,), (1,)), ((), ()))
TN = (((0,), (0,)), ((), ()))


def split(value):
    high = value.astype(BF16)
    return high, (value - high.astype(F32)).astype(BF16)


def product(left, right, dims):
    (lh, ll), (rh, rl) = left, right
    dot = functools.partial(lax.dot_general, dimension_numbers=dims, preferred_element_type=F32)
    return dot(lh, rh) + (dot(lh, rl) + dot(ll, rh))


def rotate(u, cos, sin):
    a, b = u[:, :128], u[:, 128:]
    return jnp.concatenate([a * cos - b * sin, b * cos + a * sin], axis=1)


def unrotate(u, cos, sin):
    a, b = u[:, :128], u[:, 128:]
    return jnp.concatenate([a * cos + b * sin, b * cos - a * sin], axis=1)


def inv_rms(x):
    return lax.rsqrt(jnp.mean(x * x, axis=1, keepdims=True) + EPS)


def norm_back(x, gain, d_norm):
    r = inv_rms(x)
    gd = d_norm * gain
    return r * gd - x * (r * r * r) * jnp.mean(x * gd, axis=1, keepdims=True)


class Links:
    def __init__(self, send_sems, recv_sems):
        self.sems = send_sems, recv_sems
        self.copies = {}

    def add(self, name, src, dst, device):
        i = len(self.copies)
        self.copies[name] = pltpu.make_async_remote_copy(
            src_ref=src, dst_ref=dst, send_sem=self.sems[0].at[i], recv_sem=self.sems[1].at[i],
            device_id=device, device_id_type=MESH,
        )

    def start(self, *name):
        self.copies[name].start()

    def arrived(self, *name):
        self.copies[name].wait_recv()

    def finish(self):
        for copy in self.copies.values():
            copy.wait_send()


COPIES = 72


def kernel(
    hid_h, wq_h, wk_h, wv_h, grad_h, q_gain_r, k_gain_r, seg, freq_r,
    att_o, gin_o, gq_o, gk_o, gv_o,
    hid, wq, wk, wv, grad, raw, q2, kv, wt, dpt, dqt, contrib, rkv, prev, zr,
    hz, ht_h, ht_l, dc, part, fwd, rpart, term, r1, r2, xfwd, lsem, osem, send_sems, recv_sems,
):
    s = lax.axis_index("seq")
    t = lax.axis_index("tensor")
    z, y = s // 4, lax.rem(s, 4)
    x, c = t // 2, lax.rem(t, 2)

    def at_z(d):
        return (lax.rem(z + d + 4, 4) * 4 + y, t)

    def at_y(d):
        return (z * 4 + lax.rem(y + d + 4, 4), t)

    def at_x(d):
        return (s, lax.rem(x + d + 4, 4) * 2 + c)

    mate = (s, x * 2 + 1 - c)
    barrier = pltpu.get_barrier_semaphore()
    partners = [at_z(1), at_z(2), at_z(3), at_y(1), at_y(2), at_y(3), at_x(1), at_x(2), at_x(3), mate]
    for dev in partners:
        pl.semaphore_signal(barrier, inc=1, device_id=dev, device_id_type=MESH)

    links = Links(send_sems, recv_sems)
    half = pl.ds(pl.multiple_of(c * 128, 128), 128)

    def first_col(zz):
        return ((15 * zz) // 2) * 128

    pieces_of = {0: (pl.ds(0, 128), pl.ds(128, 128)), 1: (pl.ds(0, T),)}
    for kind in (0, 1):
        for i, rows in enumerate(pieces_of[kind]):
            links.add(("kv", 4, kind, i), kv.at[0, kind, rows], kv.at[4, kind, rows], at_z(1))
            for d in (1, 2, 3):
                src = kv.at[4 * ((y + d) // 4), kind, rows]
                links.add(("kv", d, kind, i), src, kv.at[d, kind, rows], at_y(d))
        links.add(("prev", kind), prev.at[kind], zr.at[kind], at_z(-1))
        for d in (1, 2, 3):
            links.add(("back", d, kind), contrib.at[d, kind], rkv.at[d - 1, kind], at_y(-d))
    for d in (1, 2, 3):
        cols = pl.ds(pl.multiple_of(first_col(lax.rem(z + d, 4)), 128), 1024)
        links.add(("hid", d), hid.at[half, cols], hz.at[d - 1, half], at_z(d))
        links.add(("hid_mate", d), hz.at[d - 1, half], hz.at[d - 1, half], mate)
    for k in range(4):
        links.add(("core", k), term.at[1, k], r1.at[k], mate)
    for i, d in enumerate((1, 3)):
        rows = pl.ds(240 * i, 240)
        links.add(("x_fwd", d), term.at[0, 2, rows], xfwd.at[i], at_x(d))
        links.add(("x", d), term.at[0, d], r2.at[i], at_x(d))
    spans = {"q0": pl.ds(0, H), "q1": pl.ds(H, H), "k": pl.ds(2 * H, H), "v": pl.ds(3 * H, H)}
    for g, cols in spans.items():
        links.add(("dc", g, 1), dc.at[0, :, cols], dc.at[1, :, cols], at_z(1))
        links.add(("dc", g, 3), dc.at[0, :, cols], dc.at[3, :, cols], at_z(-1))
        cut = 128 if g in ("q0", "q1") else 192
        links.add(("dc2", g, 1), dc.at[1, :cut, cols], dc.at[2, :cut, cols], at_z(1))
        links.add(("dc2", g, 3), dc.at[3, cut:, cols], dc.at[2, cut:, cols], at_z(-1))
    for g in range(4):
        links.add(("fwd", g, 1), part.at[2, g, :120], fwd.at[0, g], at_y(1))
        links.add(("fwd", g, 3), part.at[2, g, 120:], fwd.at[1, g], at_y(-1))
        links.add(("sum", g, 1), part.at[1, g], rpart.at[0, g], at_y(1))
        links.add(("sum", g, 3), part.at[3, g], rpart.at[1, g], at_y(-1))

    writes = []

    def write(i, src, dst):
        copy = pltpu.make_async_copy(src, dst, osem.at[i])
        copy.start()
        writes.append(copy)

    def columns(i):
        return pl.ds(pl.multiple_of(i * CH, CH), CH)

    def local_copy(j, i):
        if j == 0:
            return pltpu.make_async_copy(hid_h.at[:, columns(i)], hid.at[:, columns(i)], lsem.at[0, i])
        src, dst = ((wk_h, wk), (wv_h, wv), (wq_h, wq))[j - 1]
        return pltpu.make_async_copy(src.at[columns(i)], dst.at[columns(i)], lsem.at[j, i])

    for i in range(NCH):
        local_copy(0, i).start()
        local_copy(1, i).start()
    for j in (2, 3):
        for i in range(NCH):
            local_copy(j, i).start()
    grad_copy = pltpu.make_async_copy(grad_h, grad, lsem.at[4, 0])
    grad_copy.start()

    place = (s * T + lax.broadcasted_iota(jnp.int32, (T, H // 2), 0)).astype(F32)
    angle = place * freq_r[...]
    cos, sin = jnp.cos(angle), jnp.sin(angle)
    q_gain, k_gain = q_gain_r[...], k_gain_r[...]

    def project(j, weight, col, load_hid, load_w):
        def step(i, acc):
            if load_hid:
                local_copy(0, i).wait()
            if load_w:
                local_copy(j, i).wait()
            left = split(hid[:, columns(i)])
            right = split(weight[columns(i), col : col + H])
            return acc + product(left, right, NN)

        return lax.fori_loop(0, NCH, step, jnp.zeros((T, H), F32))

    def send_own(kind):
        for i in range(len(pieces_of[kind])):
            links.start("kv", 4, kind, i)
        for d in (1, 2, 3):
            @pl.when(y + d < 4)
            def _():
                for i in range(len(pieces_of[kind])):
                    links.start("kv", d, kind, i)

    def send_prev(kind):
        for i in range(len(pieces_of[kind])):
            links.arrived("kv", 4, kind, i)
            for d in (1, 2, 3):
                @pl.when(y + d >= 4)
                def _():
                    links.start("kv", d, kind, i)

    def have(d, kind):
        if d in (1, 2, 3):
            for i in range(len(pieces_of[kind])):
                links.arrived("kv", d, kind, i)

    key_raw = project(1, wk, 0, True, True)
    raw[2] = key_raw
    kv[0, 0] = rotate(key_raw * inv_rms(key_raw) * k_gain, cos, sin)
    pl.semaphore_wait(barrier, len(partners))
    send_own(0)
    kv[0, 1] = project(2, wv, 0, False, True)
    send_own(1)

    def query(h, load):
        q_raw = project(3, wq, h * H, False, load)
        raw[h] = q_raw
        q2[h * T : (h + 1) * T, :] = rotate(q_raw * inv_rms(q_raw) * q_gain, cos, sin) * (H ** -0.5)

    query(0, True)
    send_prev(0)
    query(1, False)
    send_prev(1)
    grad_copy.wait()

    for d in (1, 2, 3):
        links.start("hid", d)

    def transpose_into(d, read):
        def step(i, carry):
            lanes = pl.multiple_of(i * 256, 256)
            high, low = split(read(lanes).T)
            ht_h[pl.ds(lanes, 256), d * T : (d + 1) * T] = high
            ht_l[pl.ds(lanes, 256), d * T : (d + 1) * T] = low
            return carry

        lax.fori_loop(0, 4, step, 0)

    def q_pair():
        return split(q2[...])

    def g_pair():
        return split(jnp.concatenate([grad[:, :H], grad[:, H:]], axis=0))

    row = lax.broadcasted_iota(jnp.int32, (T, 2 * T), 0)
    col = lax.rem(lax.broadcasted_iota(jnp.int32, (T, 2 * T), 1), T)

    def segments(blk):
        return seg[:, pl.ds(pl.multiple_of(blk * T, T), T)]

    seg_q = segments(s)
    seg_q = jnp.concatenate([seg_q, seg_q], axis=1)

    def weigh(d):
        seg_k = jnp.broadcast_to(segments(lax.rem(s - d + 16, 16)), (T, T)).T
        seg_k = jnp.concatenate([seg_k, seg_k], axis=1)
        dist = 256 * d + col - row
        allowed = (dist >= 0) & (dist < WINDOW) & (seg_k == seg_q) & (s - d >= 0)
        scores = product(split(kv[d, 0]), q_pair(), NT)
        weights = jnp.where(allowed, jnp.exp(scores), 0.0)
        wt[d] = weights
        return jnp.sum(weights, axis=0, keepdims=True)

    def weigh_values(d):
        d_shares = product(split(kv[d, 1]), g_pair(), NT)
        dpt[d] = d_shares
        return jnp.sum(wt[d] * d_shares, axis=0, keepdims=True)

    total = delta = jnp.zeros((1, 2 * T), F32)
    for d in (0, 4):
        total = total + weigh(d)
    for d in (0, 4):
        delta = delta + weigh_values(d)
    base = first_col(z)
    transpose_into(0, lambda lanes: hid[:, pl.ds(pl.multiple_of(base + lanes, 128), 256)])
    for d in (1, 3, 2):
        have(d, 0)
        total = total + weigh(d)
        have(d, 1)
        delta = delta + weigh_values(d)
    inverse = 1.0 / total
    delta = delta * inverse

    def back_values(d):
        shares = wt[d] * inverse
        wt[d] = shares
        contrib[d, 1] = product(split(shares), g_pair(), NN)

    def back_scores(d):
        d_scores = wt[d] * (dpt[d] - delta)
        dpt[d] = d_scores
        return product(split(kv[d, 0]), split(d_scores), TN)

    def back_keys(d):
        contrib[d, 0] = product(split(dpt[d]), q_pair(), NN)
        if d in (1, 2, 3):
            links.start("back", d, 0)

    for d in (2, 1, 3):
        back_values(d)
        links.start("back", d, 1)
    for d in (4, 0):
        wt[d] = wt[d] * inverse
    dqt[...] = back_scores(0)
    for d in (1, 2, 3, 4):
        dqt[...] = dqt[...] + back_scores(d)

    def spread(g):
        links.start("dc", g, 1)
        links.start("dc", g, 3)

    def spread_on(g):
        for d in (1, 3):
            links.arrived("dc", g, d)
            links.start("dc2", g, d)

    def gathered(g):
        for d in (1, 3):
            links.arrived("dc2", g, d)

    for h, g in ((0, "q0"), (1, "q1")):
        d_q = dqt[:, h * T : (h + 1) * T].T * (H ** -0.5)
        dc[0, :, h * H : (h + 1) * H] = norm_back(raw[h], q_gain, unrotate(d_q, cos, sin))
        spread(g)
    for d in (2, 1, 3):
        back_keys(d)
    for d in (4, 0):
        contrib[d, 1] = product(split(wt[d]), g_pair(), NN)
        back_keys(d)

    out_t = None
    for d in range(5):
        more = product(split(kv[d, 1]), split(wt[d]), TN)
        out_t = more if out_t is None else out_t + more
    q2[...] = out_t.T
    for h in (0, 1):
        write(h, q2.at[h * T : (h + 1) * T], att_o.at[:, h * H : (h + 1) * H])

    for d in (1, 2, 3):
        links.arrived("hid", d)
        links.start("hid_mate", d)

    for d in (1, 2, 3):
        if d == 3:
            spread_on("q0")
        links.arrived("hid_mate", d)
        transpose_into(d, lambda lanes: hz[d - 1, :, pl.ds(lanes, 256)])

    weights = [(wq, 0), (wq, H), (wk, 0), (wv, 0)]

    def input_part(k, core, grads):
        rows = pl.ds(pl.multiple_of((2 * lax.rem(x + k, 4) + core) * 480, 32), 480)
        acc = None
        for g, grad_g in grads.items():
            w, first = weights[g]
            one = product(split(w[rows, first : first + H]), grad_g, NT)
            acc = one if acc is None else acc + one
        return acc

    q_own = {g: split(dc[0, :, g * H : (g + 1) * H]) for g in (0, 1)}
    for k in range(4):
        term[0, k] = input_part(k, c, q_own)
        if k == 1:
            spread_on("q1")
        term[1, k] = input_part(k, 1 - c, q_own)

    def collect(kind):
        mine, before = contrib[0, kind], contrib[4, kind]
        for d in (1, 2, 3):
            links.arrived("back", d, kind)
            got = rkv[d - 1, kind]
            inside = jnp.where(y + d < 4, 1.0, 0.0).astype(F32)
            mine = mine + inside * got
            before = before + (1.0 - inside) * got
        prev[kind] = before
        contrib[0, kind] = mine
        links.start("prev", kind)

    collect(1)

    off = lax.rem(z, 2) * 64

    def send_far(g):
        links.start("fwd", g, 1)
        links.start("fwd", g, 3)

    def partial(g):
        pieces = [split(dc[k, :, g * H : (g + 1) * H]) for k in range(4)]
        right = tuple(jnp.concatenate([p[i] for p in pieces], axis=0) for i in (0, 1))
        for d in (2, 1, 3, 0):
            rows = pl.ds(pl.multiple_of(off + 240 * lax.rem(y + d, 4), 16), 240)
            part[d, g] = product((ht_h[rows, :], ht_l[rows, :]), right, NN)
            if d == 2 and g > 1:
                send_far(g)

    def pass_on(g):
        links.arrived("fwd", g, 1)
        part[1, g, :120] = part[1, g, :120] + fwd[0, g]
        links.start("sum", g, 1)
        links.arrived("fwd", g, 3)
        part[3, g, 120:] = part[3, g, 120:] + fwd[1, g]
        links.start("sum", g, 3)

    def summed(g):
        links.arrived("sum", g, 1)
        links.arrived("sum", g, 3)
        part[0, g] = part[0, g] + (rpart[0, g] + rpart[1, g])
        dst = (gq_o.at[:, :H], gq_o.at[:, H:], gk_o, gv_o)[g]
        write(2 + g, part.at[0, g], dst)

    gathered("q0")
    partial(0)
    gathered("q1")
    partial(1)
    collect(0)
    send_far(0)
    send_far(1)

    links.arrived("prev", 1)
    dc[0, :, 3 * H : 4 * H] = contrib[0, 1] + zr[1]
    spread("v")
    links.arrived("prev", 0)
    d_key = unrotate(contrib[0, 0] + zr[0], cos, sin)
    dc[0, :, 2 * H : 3 * H] = norm_back(raw[2], k_gain, d_key)
    spread("k")
    pass_on(0)
    pass_on(1)

    kv_own = {g: split(dc[0, :, g * H : (g + 1) * H]) for g in (2, 3)}

    def other(k):
        term[1, k] = term[1, k] + input_part(k, 1 - c, kv_own)
        links.start("core", k)

    def both(k):
        mine = term[0, k] + input_part(k, c, kv_own)
        links.arrived("core", k)
        term[0, k] = mine + r1[k]

    other(2)
    other(1)
    both(2)
    for d in (1, 3):
        links.start("x_fwd", d)
    spread_on("v")
    other(3)
    other(0)
    for k in (1, 3, 0):
        both(k)

    gathered("v")
    partial(3)
    spread_on("k")
    for i, d in enumerate((1, 3)):
        links.arrived("x_fwd", d)
        rows = pl.ds(240 * i, 240)
        term[0, d, rows] = term[0, d, rows] + xfwd[i]
        links.start("x", d)
    gathered("k")
    partial(2)
    pass_on(3)
    pass_on(2)

    summed(0)
    summed(1)
    links.arrived("x", 1)
    links.arrived("x", 3)
    term[0, 0] = term[0, 0] + (r2[0] + r2[1])
    write(6, term.at[0, 0], gin_o)
    summed(3)
    summed(2)
    for copy in writes:
        copy.wait()
    links.finish()


def hand_over(*refs):
    ins, outs, held, sems = refs[:5], refs[5:10], refs[10:15], refs[15]
    loads = [pltpu.make_async_copy(ins[i], held[i], sems.at[0, i]) for i in range(5)]
    stores = [pltpu.make_async_copy(held[i], outs[i], sems.at[1, i]) for i in range(5)]
    for load in loads:
        load.start()
    for load, store in zip(loads, stores):
        load.wait()
        store.start()
    for store in stores:
        store.wait()


def local(hidden_in, query_proj, key_proj, value_proj, query_gain, key_gain, segment_ids, grad_out):
    frequency = np.power(10000.0, -2.0 * np.arange(H // 2) / H).astype(np.float32)[None, :]
    vmem = pl.BlockSpec(memory_space=pltpu.VMEM)
    hbm = pl.BlockSpec(memory_space=pl.ANY)
    V, S = pltpu.VMEM, pltpu.SemaphoreType.DMA
    shape = jax.ShapeDtypeStruct
    outs = (
        shape((T, 512), F32), shape((480, T), F32), shape((240, 512), F32), shape((240, 256), F32), shape((240, 256), F32),
    )
    results = pl.pallas_call(
        kernel,
        out_shape=outs,
        in_specs=[hbm] * 5 + [vmem] * 4,
        out_specs=(hbm,) * 5,
        scratch_shapes=[
            V((T, D), F32), V((D, 512), F32), V((D, 256), F32), V((D, 256), F32), V((T, 512), F32),
            V((3, T, H), F32), V((2 * T, H), F32), V((5, 2, T, H), F32), V((5, T, 2 * T), F32), V((5, T, 2 * T), F32),
            V((H, 2 * T), F32), V((5, 2, T, H), F32), V((3, 2, T, H), F32), V((2, T, H), F32), V((2, T, H), F32),
            V((3, T, 1024), F32), V((1024, 1024), BF16), V((1024, 1024), BF16), V((4, T, 1024), F32),
            V((4, 4, 240, H), F32), V((2, 4, 120, H), F32), V((2, 4, 240, H), F32),
            V((2, 4, 480, T), F32), V((4, 480, T), F32), V((2, 480, T), F32), V((2, 240, T), F32),
            S((5, NCH)), S((7,)), S((COPIES,)), S((COPIES,)),
        ],
        compiler_params=pltpu.CompilerParams(collective_id=0, has_side_effects=True, vmem_limit_bytes=63 << 20),
        cost_estimate=pl.CostEstimate(flops=24_000_000_000, bytes_accessed=40_000_000, transcendentals=700_000),
    )(
        hidden_in, query_proj, key_proj, value_proj, grad_out,
        query_gain.reshape(1, H), key_gain.reshape(1, H), segment_ids.reshape(1, -1), jnp.asarray(frequency),
    )
    attended, grad_in, grad_query, grad_key, grad_value = pl.pallas_call(
        hand_over, out_shape=outs, in_specs=[hbm] * 5, out_specs=(hbm,) * 5,
        scratch_shapes=[V(out.shape, F32) for out in outs] + [S((2, 5))],
    )(*results)
    return attended, grad_in.T, grad_query, grad_key, grad_value


def solution(mesh):
    return jax.shard_map(
        local,
        mesh=mesh,
        in_specs=(
            P("seq", None), P(None, "tensor"), P(None, "tensor"), P(None, "tensor"), P(), P(), P(), P("seq", "tensor"),
        ),
        out_specs=(P("seq", "tensor"),) * 5,
        check_vma=False,
    )
```

```python
import functools

import jax
import jax.numpy as jnp
import numpy as np
from jax import lax
from jax.experimental import pallas as pl
from jax.experimental.pallas import tpu as pltpu
from jax.sharding import PartitionSpec as P

MESH = pl.DeviceIdType.MESH
WINDOW = 1024
EPS = 1e-06
T = 256
H = 256
D = 3840
NCH = 5
CH = D // NCH
F32, BF16 = jnp.float32, jnp.bfloat16

NN = (((1,), (0,)), ((), ()))
NT = (((1,), (1,)), ((), ()))
TN = (((0,), (0,)), ((), ()))


def split(value):
    high = value.astype(BF16)
    return high, (value - high.astype(F32)).astype(BF16)


def product(left, right, dims):
    (lh, ll), (rh, rl) = left, right
    dot = functools.partial(lax.dot_general, dimension_numbers=dims, preferred_element_type=F32)
    return dot(lh, rh) + (dot(lh, rl) + dot(ll, rh))


def rotate(u, cos, sin):
    a, b = u[:, :128], u[:, 128:]
    return jnp.concatenate([a * cos - b * sin, b * cos + a * sin], axis=1)


def unrotate(u, cos, sin):
    a, b = u[:, :128], u[:, 128:]
    return jnp.concatenate([a * cos + b * sin, b * cos - a * sin], axis=1)


def inv_rms(x):
    return lax.rsqrt(jnp.mean(x * x, axis=1, keepdims=True) + EPS)


def norm_back(x, gain, d_norm):
    r = inv_rms(x)
    gd = d_norm * gain
    return r * gd - x * (r * r * r) * jnp.mean(x * gd, axis=1, keepdims=True)


class Links:
    def __init__(self, send_sems, recv_sems):
        self.sems = send_sems, recv_sems
        self.copies = {}

    def add(self, name, src, dst, device):
        i = len(self.copies)
        self.copies[name] = pltpu.make_async_remote_copy(
            src_ref=src, dst_ref=dst, send_sem=self.sems[0].at[i], recv_sem=self.sems[1].at[i],
            device_id=device, device_id_type=MESH,
        )

    def start(self, *name):
        self.copies[name].start()

    def arrived(self, *name):
        self.copies[name].wait_recv()

    def finish(self):
        for copy in self.copies.values():
            copy.wait_send()


COPIES = 72


def kernel(
    hid_h, wq_h, wk_h, wv_h, grad_h, q_gain_r, k_gain_r, seg, freq_r,
    att_o, gin_o, gq_o, gk_o, gv_o,
    hid, wq, wk, wv, grad, raw, q2, kv, wt, dpt, dqt, contrib, rkv, prev, zr,
    hz, ht_h, ht_l, dc, part, fwd, rpart, term, r1, r2, xfwd, lsem, osem, send_sems, recv_sems,
):
    s = lax.axis_index("seq")
    t = lax.axis_index("tensor")
    z, y = s // 4, lax.rem(s, 4)
    x, c = t // 2, lax.rem(t, 2)

    def at_z(d):
        return (lax.rem(z + d + 4, 4) * 4 + y, t)

    def at_y(d):
        return (z * 4 + lax.rem(y + d + 4, 4), t)

    def at_x(d):
        return (s, lax.rem(x + d + 4, 4) * 2 + c)

    mate = (s, x * 2 + 1 - c)
    barrier = pltpu.get_barrier_semaphore()
    partners = [at_z(1), at_z(2), at_z(3), at_y(1), at_y(2), at_y(3), at_x(1), at_x(2), at_x(3), mate]
    for dev in partners:
        pl.semaphore_signal(barrier, inc=1, device_id=dev, device_id_type=MESH)

    links = Links(send_sems, recv_sems)
    half = pl.ds(pl.multiple_of(c * 128, 128), 128)

    def first_col(zz):
        return ((15 * zz) // 2) * 128

    pieces_of = {0: (pl.ds(0, 128), pl.ds(128, 128)), 1: (pl.ds(0, T),)}
    for kind in (0, 1):
        for i, rows in enumerate(pieces_of[kind]):
            links.add(("kv", 4, kind, i), kv.at[0, kind, rows], kv.at[4, kind, rows], at_z(1))
            for d in (1, 2, 3):
                src = kv.at[4 * ((y + d) // 4), kind, rows]
                links.add(("kv", d, kind, i), src, kv.at[d, kind, rows], at_y(d))
        links.add(("prev", kind), prev.at[kind], zr.at[kind], at_z(-1))
        for d in (1, 2, 3):
            links.add(("back", d, kind), contrib.at[d, kind], rkv.at[d - 1, kind], at_y(-d))
    for d in (1, 2, 3):
        cols = pl.ds(pl.multiple_of(first_col(lax.rem(z + d, 4)), 128), 1024)
        links.add(("hid", d), hid.at[half, cols], hz.at[d - 1, half], at_z(d))
        links.add(("hid_mate", d), hz.at[d - 1, half], hz.at[d - 1, half], mate)
    for k in range(4):
        links.add(("core", k), term.at[1, k], r1.at[k], mate)
    for i, d in enumerate((1, 3)):
        rows = pl.ds(240 * i, 240)
        links.add(("x_fwd", d), term.at[0, 2, rows], xfwd.at[i], at_x(d))
        links.add(("x", d), term.at[0, d], r2.at[i], at_x(d))
    spans = {"q0": pl.ds(0, H), "q1": pl.ds(H, H), "k": pl.ds(2 * H, H), "v": pl.ds(3 * H, H)}
    for g, cols in spans.items():
        links.add(("dc", g, 1), dc.at[0, :, cols], dc.at[1, :, cols], at_z(1))
        links.add(("dc", g, 3), dc.at[0, :, cols], dc.at[3, :, cols], at_z(-1))
        cut = 128 if g in ("q0", "q1") else 192
        links.add(("dc2", g, 1), dc.at[1, :cut, cols], dc.at[2, :cut, cols], at_z(1))
        links.add(("dc2", g, 3), dc.at[3, cut:, cols], dc.at[2, cut:, cols], at_z(-1))
    for g in range(4):
        links.add(("fwd", g, 1), part.at[2, g, :120], fwd.at[0, g], at_y(1))
        links.add(("fwd", g, 3), part.at[2, g, 120:], fwd.at[1, g], at_y(-1))
        links.add(("sum", g, 1), part.at[1, g], rpart.at[0, g], at_y(1))
        links.add(("sum", g, 3), part.at[3, g], rpart.at[1, g], at_y(-1))

    writes = []

    def write(i, src, dst):
        copy = pltpu.make_async_copy(src, dst, osem.at[i])
        copy.start()
        writes.append(copy)

    def columns(i):
        return pl.ds(pl.multiple_of(i * CH, CH), CH)

    def local_copy(j, i):
        if j == 0:
            return pltpu.make_async_copy(hid_h.at[:, columns(i)], hid.at[:, columns(i)], lsem.at[0, i])
        src, dst = ((wk_h, wk), (wv_h, wv), (wq_h, wq))[j - 1]
        return pltpu.make_async_copy(src.at[columns(i)], dst.at[columns(i)], lsem.at[j, i])

    for i in range(NCH):
        local_copy(0, i).start()
        local_copy(1, i).start()
    for j in (2, 3):
        for i in range(NCH):
            local_copy(j, i).start()
    grad_copy = pltpu.make_async_copy(grad_h, grad, lsem.at[4, 0])
    grad_copy.start()

    place = (s * T + lax.broadcasted_iota(jnp.int32, (T, H // 2), 0)).astype(F32)
    angle = place * freq_r[...]
    cos, sin = jnp.cos(angle), jnp.sin(angle)
    q_gain, k_gain = q_gain_r[...], k_gain_r[...]

    def project(j, weight, col, load_hid, load_w):
        def step(i, acc):
            if load_hid:
                local_copy(0, i).wait()
            if load_w:
                local_copy(j, i).wait()
            left = split(hid[:, columns(i)])
            right = split(weight[columns(i), col : col + H])
            return acc + product(left, right, NN)

        return lax.fori_loop(0, NCH, step, jnp.zeros((T, H), F32))

    def send_own(kind):
        for i in range(len(pieces_of[kind])):
            links.start("kv", 4, kind, i)
        for d in (1, 2, 3):
            @pl.when(y + d < 4)
            def _():
                for i in range(len(pieces_of[kind])):
                    links.start("kv", d, kind, i)

    def send_prev(kind):
        for i in range(len(pieces_of[kind])):
            links.arrived("kv", 4, kind, i)
            for d in (1, 2, 3):
                @pl.when(y + d >= 4)
                def _():
                    links.start("kv", d, kind, i)

    def have(d, kind):
        if d in (1, 2, 3):
            for i in range(len(pieces_of[kind])):
                links.arrived("kv", d, kind, i)

    key_raw = project(1, wk, 0, True, True)
    raw[2] = key_raw
    kv[0, 0] = rotate(key_raw * inv_rms(key_raw) * k_gain, cos, sin)
    pl.semaphore_wait(barrier, len(partners))
    send_own(0)
    kv[0, 1] = project(2, wv, 0, False, True)
    send_own(1)

    def query(h, load):
        q_raw = project(3, wq, h * H, False, load)
        raw[h] = q_raw
        q2[h * T : (h + 1) * T, :] = rotate(q_raw * inv_rms(q_raw) * q_gain, cos, sin) * (H ** -0.5)

    query(0, True)
    send_prev(0)
    query(1, False)
    send_prev(1)
    grad_copy.wait()

    for d in (1, 2, 3):
        links.start("hid", d)

    def transpose_into(d, read):
        def step(i, carry):
            lanes = pl.multiple_of(i * 256, 256)
            high, low = split(read(lanes).T)
            ht_h[pl.ds(lanes, 256), d * T : (d + 1) * T] = high
            ht_l[pl.ds(lanes, 256), d * T : (d + 1) * T] = low
            return carry

        lax.fori_loop(0, 4, step, 0)

    def q_pair():
        return split(q2[...])

    def g_pair():
        return split(jnp.concatenate([grad[:, :H], grad[:, H:]], axis=0))

    row = lax.broadcasted_iota(jnp.int32, (T, 2 * T), 0)
    col = lax.rem(lax.broadcasted_iota(jnp.int32, (T, 2 * T), 1), T)

    def segments(blk):
        return seg[:, pl.ds(pl.multiple_of(blk * T, T), T)]

    seg_q = segments(s)
    seg_q = jnp.concatenate([seg_q, seg_q], axis=1)

    def weigh(d):
        seg_k = jnp.broadcast_to(segments(lax.rem(s - d + 16, 16)), (T, T)).T
        seg_k = jnp.concatenate([seg_k, seg_k], axis=1)
        dist = 256 * d + col - row
        allowed = (dist >= 0) & (dist < WINDOW) & (seg_k == seg_q) & (s - d >= 0)
        scores = product(split(kv[d, 0]), q_pair(), NT)
        weights = jnp.where(allowed, jnp.exp(scores), 0.0)
        wt[d] = weights
        return jnp.sum(weights, axis=0, keepdims=True)

    def weigh_values(d):
        d_shares = product(split(kv[d, 1]), g_pair(), NT)
        dpt[d] = d_shares
        return jnp.sum(wt[d] * d_shares, axis=0, keepdims=True)

    total = delta = jnp.zeros((1, 2 * T), F32)
    for d in (0, 4):
        total = total + weigh(d)
    for d in (0, 4):
        delta = delta + weigh_values(d)
    base = first_col(z)
    transpose_into(0, lambda lanes: hid[:, pl.ds(pl.multiple_of(base + lanes, 128), 256)])
    for d in (1, 3, 2):
        have(d, 0)
        total = total + weigh(d)
        have(d, 1)
        delta = delta + weigh_values(d)
    inverse = 1.0 / total
    delta = delta * inverse

    def back_values(d):
        shares = wt[d] * inverse
        wt[d] = shares
        contrib[d, 1] = product(split(shares), g_pair(), NN)

    def back_scores(d):
        d_scores = wt[d] * (dpt[d] - delta)
        dpt[d] = d_scores
        return product(split(kv[d, 0]), split(d_scores), TN)

    def back_keys(d):
        contrib[d, 0] = product(split(dpt[d]), q_pair(), NN)
        if d in (1, 2, 3):
            links.start("back", d, 0)

    for d in (2, 1, 3):
        back_values(d)
        links.start("back", d, 1)
    for d in (4, 0):
        wt[d] = wt[d] * inverse
    dqt[...] = back_scores(0)
    for d in (1, 2, 3, 4):
        dqt[...] = dqt[...] + back_scores(d)

    def spread(g):
        links.start("dc", g, 1)
        links.start("dc", g, 3)

    def spread_on(g):
        for d in (1, 3):
            links.arrived("dc", g, d)
            links.start("dc2", g, d)

    def gathered(g):
        for d in (1, 3):
            links.arrived("dc2", g, d)

    for h, g in ((0, "q0"), (1, "q1")):
        d_q = dqt[:, h * T : (h + 1) * T].T * (H ** -0.5)
        dc[0, :, h * H : (h + 1) * H] = norm_back(raw[h], q_gain, unrotate(d_q, cos, sin))
        spread(g)
    for d in (2, 1, 3):
        back_keys(d)
    for d in (4, 0):
        contrib[d, 1] = product(split(wt[d]), g_pair(), NN)
        back_keys(d)

    for d in (1, 2, 3):
        links.arrived("hid", d)
        links.start("hid_mate", d)

    for d in (1, 2, 3):
        if d == 3:
            spread_on("q0")
        links.arrived("hid_mate", d)
        transpose_into(d, lambda lanes: hz[d - 1, :, pl.ds(lanes, 256)])

    weights = [(wq, 0), (wq, H), (wk, 0), (wv, 0)]

    def input_part(k, core, grads):
        rows = pl.ds(pl.multiple_of((2 * lax.rem(x + k, 4) + core) * 480, 32), 480)
        acc = None
        for g, grad_g in grads.items():
            w, first = weights[g]
            one = product(split(w[rows, first : first + H]), grad_g, NT)
            acc = one if acc is None else acc + one
        return acc

    q_own = {g: split(dc[0, :, g * H : (g + 1) * H]) for g in (0, 1)}
    for k in range(4):
        term[0, k] = input_part(k, c, q_own)
        if k == 1:
            spread_on("q1")
        term[1, k] = input_part(k, 1 - c, q_own)

    def collect(kind):
        mine, before = contrib[0, kind], contrib[4, kind]
        for d in (1, 2, 3):
            links.arrived("back", d, kind)
            got = rkv[d - 1, kind]
            inside = jnp.where(y + d < 4, 1.0, 0.0).astype(F32)
            mine = mine + inside * got
            before = before + (1.0 - inside) * got
        prev[kind] = before
        contrib[0, kind] = mine
        links.start("prev", kind)

    collect(1)

    off = lax.rem(z, 2) * 64

    def send_far(g):
        links.start("fwd", g, 1)
        links.start("fwd", g, 3)

    def partial(g):
        pieces = [split(dc[k, :, g * H : (g + 1) * H]) for k in range(4)]
        right = tuple(jnp.concatenate([p[i] for p in pieces], axis=0) for i in (0, 1))
        for d in (2, 1, 3, 0):
            rows = pl.ds(pl.multiple_of(off + 240 * lax.rem(y + d, 4), 16), 240)
            part[d, g] = product((ht_h[rows, :], ht_l[rows, :]), right, NN)
            if d == 2 and g > 1:
                send_far(g)

    def pass_on(g):
        links.arrived("fwd", g, 1)
        part[1, g, :120] = part[1, g, :120] + fwd[0, g]
        links.start("sum", g, 1)
        links.arrived("fwd", g, 3)
        part[3, g, 120:] = part[3, g, 120:] + fwd[1, g]
        links.start("sum", g, 3)

    def summed(g):
        links.arrived("sum", g, 1)
        links.arrived("sum", g, 3)
        part[0, g] = part[0, g] + (rpart[0, g] + rpart[1, g])
        dst = (gq_o.at[:, :H], gq_o.at[:, H:], gk_o, gv_o)[g]
        write(2 + g, part.at[0, g], dst)

    gathered("q0")
    partial(0)
    gathered("q1")
    partial(1)
    out_t = None
    for d in range(5):
        more = product(split(kv[d, 1]), split(wt[d]), TN)
        out_t = more if out_t is None else out_t + more
    q2[...] = out_t.T
    for h in (0, 1):
        write(h, q2.at[h * T : (h + 1) * T], att_o.at[:, h * H : (h + 1) * H])

    collect(0)
    send_far(0)
    send_far(1)

    links.arrived("prev", 1)
    dc[0, :, 3 * H : 4 * H] = contrib[0, 1] + zr[1]
    spread("v")
    links.arrived("prev", 0)
    d_key = unrotate(contrib[0, 0] + zr[0], cos, sin)
    dc[0, :, 2 * H : 3 * H] = norm_back(raw[2], k_gain, d_key)
    spread("k")
    pass_on(0)
    pass_on(1)

    kv_own = {g: split(dc[0, :, g * H : (g + 1) * H]) for g in (2, 3)}

    def other(k):
        term[1, k] = term[1, k] + input_part(k, 1 - c, kv_own)
        links.start("core", k)

    def both(k):
        mine = term[0, k] + input_part(k, c, kv_own)
        links.arrived("core", k)
        term[0, k] = mine + r1[k]

    other(2)
    other(1)
    both(2)
    for d in (1, 3):
        links.start("x_fwd", d)
    spread_on("v")
    other(3)
    other(0)
    for k in (1, 3, 0):
        both(k)

    gathered("v")
    partial(3)
    spread_on("k")
    for i, d in enumerate((1, 3)):
        links.arrived("x_fwd", d)
        rows = pl.ds(240 * i, 240)
        term[0, d, rows] = term[0, d, rows] + xfwd[i]
        links.start("x", d)
    gathered("k")
    partial(2)
    pass_on(3)
    pass_on(2)

    summed(0)
    summed(1)
    links.arrived("x", 1)
    links.arrived("x", 3)
    term[0, 0] = term[0, 0] + (r2[0] + r2[1])
    write(6, term.at[0, 0], gin_o)
    summed(3)
    summed(2)
    for copy in writes:
        copy.wait()
    links.finish()


def hand_over(*refs):
    ins, outs, held, sems = refs[:5], refs[5:10], refs[10:15], refs[15]
    loads = [pltpu.make_async_copy(ins[i], held[i], sems.at[0, i]) for i in range(5)]
    stores = [pltpu.make_async_copy(held[i], outs[i], sems.at[1, i]) for i in range(5)]
    for load in loads:
        load.start()
    for load, store in zip(loads, stores):
        load.wait()
        store.start()
    for store in stores:
        store.wait()


def local(hidden_in, query_proj, key_proj, value_proj, query_gain, key_gain, segment_ids, grad_out):
    frequency = np.power(10000.0, -2.0 * np.arange(H // 2) / H).astype(np.float32)[None, :]
    vmem = pl.BlockSpec(memory_space=pltpu.VMEM)
    hbm = pl.BlockSpec(memory_space=pl.ANY)
    V, S = pltpu.VMEM, pltpu.SemaphoreType.DMA
    shape = jax.ShapeDtypeStruct
    outs = (
        shape((T, 512), F32), shape((480, T), F32), shape((240, 512), F32), shape((240, 256), F32), shape((240, 256), F32),
    )
    results = pl.pallas_call(
        kernel,
        out_shape=outs,
        in_specs=[hbm] * 5 + [vmem] * 4,
        out_specs=(hbm,) * 5,
        scratch_shapes=[
            V((T, D), F32), V((D, 512), F32), V((D, 256), F32), V((D, 256), F32), V((T, 512), F32),
            V((3, T, H), F32), V((2 * T, H), F32), V((5, 2, T, H), F32), V((5, T, 2 * T), F32), V((5, T, 2 * T), F32),
            V((H, 2 * T), F32), V((5, 2, T, H), F32), V((3, 2, T, H), F32), V((2, T, H), F32), V((2, T, H), F32),
            V((3, T, 1024), F32), V((1024, 1024), BF16), V((1024, 1024), BF16), V((4, T, 1024), F32),
            V((4, 4, 240, H), F32), V((2, 4, 120, H), F32), V((2, 4, 240, H), F32),
            V((2, 4, 480, T), F32), V((4, 480, T), F32), V((2, 480, T), F32), V((2, 240, T), F32),
            S((5, NCH)), S((7,)), S((COPIES,)), S((COPIES,)),
        ],
        compiler_params=pltpu.CompilerParams(collective_id=0, has_side_effects=True, vmem_limit_bytes=63 << 20),
        cost_estimate=pl.CostEstimate(flops=24_000_000_000, bytes_accessed=40_000_000, transcendentals=700_000),
    )(
        hidden_in, query_proj, key_proj, value_proj, grad_out,
        query_gain.reshape(1, H), key_gain.reshape(1, H), segment_ids.reshape(1, -1), jnp.asarray(frequency),
    )
    attended, grad_in, grad_query, grad_key, grad_value = pl.pallas_call(
        hand_over, out_shape=outs, in_specs=[hbm] * 5, out_specs=(hbm,) * 5,
        scratch_shapes=[V(out.shape, F32) for out in outs] + [S((2, 5))],
    )(*results)
    return attended, grad_in.T, grad_query, grad_key, grad_value


def solution(mesh):
    return jax.shard_map(
        local,
        mesh=mesh,
        in_specs=(
            P("seq", None), P(None, "tensor"), P(None, "tensor"), P(None, "tensor"), P(), P(), P(), P("seq", "tensor"),
        ),
        out_specs=(P("seq", "tensor"),) * 5,
        check_vma=False,
    )
```
